32 devices in a mesh: visit: 8 (over z, core), grp: 4 (over y, x).
Axes of the slice: x: 2, y: 2, z: 4, core: 2. Of those that a mesh axis runs over, the one named last changes fastest.
Arguments:
- coadd_tiles: float32 [2048, 8192], P('visit', 'grp'), may hold values from -9 to 9
- science: float32 [2048, 8192], P('visit', 'grp'), may hold values from -16 to 16
- correlation: int32 [8], P('visit'), may hold values from 0 to 7, as said below
- offset: int32 [8], P('visit'), may hold values from 10 to 246
Outputs:
- difference: float32 [2048, 8192], P('visit', 'grp')
- significance: float32 [2048, 8192], P('visit', 'grp')
- match_coef: float32 [8, 6], P('visit')
The draws below stay inside these ranges and needn't reach their ends.
Inputs may be any that keep to these rules, and one draw needn't show every extreme that they name: correlation is a permutation of 0 .. 7.
All inputs are finite; a program needn't handle non-finite values.
Results may differ from the reference program's by a relative error of at most 0.0003.
Values sent between devices are 32-bit elements; how exact they have to be, the bound alone decides.
A program may use at most 128 MiB of HBM per device.

```python
import jax
import jax.numpy as jnp
from jax import lax

ROWS = 256
COLS = 2048
KER_HALF = 10
BASIS = 5
FILT_HALF = 6
N_VISIT = 8
N_GRP = 4


def sky_tiles(key):
    layout = (N_VISIT * ROWS, N_GRP * COLS)
    values = jax.random.truncated_normal(jax.random.fold_in(key, 11), -5.0, 5.0, layout, jnp.float32)
    stripe = (jnp.arange(N_GRP * COLS) // COLS).astype(jnp.float32)
    amplitude = 3.0 ** (0.5 * stripe / max(N_GRP - 1, 1))
    return values * amplitude[None, :]


def sky_table(key):
    ordering = jax.random.permutation(jax.random.fold_in(key, 12), N_VISIT).astype(jnp.int32)
    shifts = jax.random.randint(jax.random.fold_in(key, 13), (N_VISIT,), KER_HALF, ROWS - KER_HALF + 1).astype(jnp.int32)
    chosen = jax.random.permutation(jax.random.fold_in(key, 18), N_VISIT).astype(jnp.int32)
    shifts = shifts.at[chosen[0]].set(ROWS - KER_HALF)
    shifts = shifts.at[chosen[1]].set(KER_HALF)
    return (ordering, shifts.astype(jnp.int32))


def draw_coadd_tiles(key, part):
    return sky_tiles(key)


def draw_correlation(key, part):
    return sky_table(key)[0]


def draw_offset(key, part):
    return sky_table(key)[1]


def draw_science(key, part):
    coadd_tiles = sky_tiles(key)
    ordering, shifts = sky_table(key)
    padded = jnp.pad(coadd_tiles, ((0, 0), (KER_HALF, KER_HALF)))
    spreads = jax.random.uniform(jax.random.fold_in(key, 14), (N_VISIT,), jnp.float32, 1.2, 2.6)
    gains = jnp.exp(jax.random.uniform(jax.random.fold_in(key, 15), (N_VISIT, N_GRP), jnp.float32, jnp.log(0.6), jnp.log(1.6)))
    levels = jax.random.uniform(jax.random.fold_in(key, 16), (N_VISIT, N_GRP), jnp.float32, -0.5, 0.5)
    noise = 0.1 * jax.random.truncated_normal(jax.random.fold_in(key, 17), -5.0, 5.0, (N_VISIT, ROWS, N_GRP * COLS), jnp.float32)
    points = jnp.arange(-KER_HALF, KER_HALF + 1).astype(jnp.float32)

    def exposure(inputs):
        tile_id, shift_rows, spread = inputs
        rows_index = (tile_id * ROWS + shift_rows - KER_HALF + jnp.arange(ROWS + 2 * KER_HALF).astype(jnp.int32)) % (N_VISIT * ROWS)
        window = jnp.take(padded, rows_index.astype(jnp.int32), axis=0)
        kernel_taps = jnp.exp(-points * points / (2.0 * spread * spread))
        kernel_taps = kernel_taps / jnp.sum(kernel_taps)
        blurred = lax.conv_general_dilated(window[None, None], kernel_taps[None, None, None, :], (1, 1), 'VALID')
        blurred = lax.conv_general_dilated(blurred, kernel_taps[None, None, :, None], (1, 1), 'VALID')
        return blurred[0, 0]
    blurred = lax.map(exposure, (ordering, shifts, spreads))
    stripe = jnp.arange(N_GRP * COLS) // COLS
    gain_cols = jnp.take(gains, stripe, axis=1)
    level_cols = jnp.take(levels, stripe, axis=1)
    result = blurred * gain_cols[:, None, :] + level_cols[:, None, :] + noise
    return result.reshape(N_VISIT * ROWS, N_GRP * COLS)


def setup_inputs(seed: int = 0) -> dict:
    keys = jax.random.split(jax.random.key(seed), 5)
    coadd_tiles = draw_coadd_tiles(jax.random.fold_in(keys[4], 71), 0)
    science = draw_science(jax.random.fold_in(keys[4], 71), 0)
    correlation = draw_correlation(jax.random.fold_in(keys[4], 71), 0)
    offset = draw_offset(jax.random.fold_in(keys[4], 71), 0)
    return dict(coadd_tiles=coadd_tiles, science=science, correlation=correlation, offset=offset)


ridge = 0.05
epsilon = 1e-06

def gauss_taps(spread, half_width):
    points = jnp.arange(-half_width, half_width + 1).astype(jnp.float32)
    return jnp.exp(-points * points / (2.0 * spread * spread))

def basis_taps():
    points = jnp.arange(-KER_HALF, KER_HALF + 1).astype(jnp.float32)
    narrow = gauss_taps(1.0, KER_HALF)
    middle = gauss_taps(1.8, KER_HALF)
    wide_gauss = gauss_taps(3.2, KER_HALF)
    slope_taps = points * middle / 1.8
    row_taps = jnp.stack([narrow, middle, wide_gauss, slope_taps, middle])
    col_taps = jnp.stack([narrow, middle, wide_gauss, middle, slope_taps])
    scales = jnp.sqrt(lax.optimization_barrier(jnp.sum(row_taps * row_taps, 1)) * lax.optimization_barrier(jnp.sum(col_taps * col_taps, 1)))
    return (row_taps / scales[:, None], col_taps)

def filter_taps():
    smooth = gauss_taps(2.0, FILT_HALF)
    return smooth / jnp.sqrt(jnp.sum(smooth * smooth))

def along_cols_ref(image_in, kernel_taps):
    result = lax.conv_general_dilated(image_in[None, None], kernel_taps[:, None, None, :], (1, 1), 'VALID', precision=lax.Precision.HIGHEST)
    return result[0]

def along_rows_ref(layers, kernel_taps):
    result = lax.conv_general_dilated(layers[None], kernel_taps[:, None, :, None], (1, 1), 'VALID', feature_group_count=layers.shape[0], precision=lax.Precision.HIGHEST)
    return result[0]

def build_normal(gram_matrix, basis_sums, counted):
    upper_rows = jnp.concatenate([gram_matrix, basis_sums[:, None]], 1)
    lower_row = jnp.concatenate([basis_sums, jnp.array([counted], jnp.float32)])[None]
    return jnp.concatenate([upper_rows, lower_row], 0) / counted + ridge * jnp.eye(BASIS + 1, dtype=jnp.float32)

def reference(coadd_tiles, science, correlation, offset):
    row_taps, col_taps = basis_taps()
    smooth = filter_taps()[None]
    strip_rows = N_VISIT * ROWS
    padded = jnp.pad(coadd_tiles, ((0, 0), (KER_HALF, KER_HALF)))
    counted = float(ROWS * COLS * N_GRP)

    def exposure(inputs):
        tile_id, shift_rows, science_rows = inputs
        first_row = tile_id * ROWS + shift_rows - KER_HALF
        rows_index = (first_row + jnp.arange(ROWS + 2 * KER_HALF).astype(jnp.int32)) % strip_rows
        window = jnp.take(padded, rows_index.astype(jnp.int32), axis=0)
        matched = along_rows_ref(along_cols_ref(window, col_taps), row_taps)
        basis_flat = matched.reshape(BASIS, -1)
        gram_matrix = jnp.dot(basis_flat, basis_flat.T, precision=lax.Precision.HIGHEST)
        basis_sums = lax.optimization_barrier(jnp.sum(basis_flat, 1))
        projection = jnp.dot(basis_flat, science_rows.reshape(-1), precision=lax.Precision.HIGHEST)
        science_total = jnp.sum(science_rows)
        normal = build_normal(gram_matrix, basis_sums, counted)
        rhs_vector = jnp.concatenate([projection, science_total[None]]) / counted
        coefficients = jnp.linalg.solve(normal, rhs_vector)
        difference = science_rows - lax.optimization_barrier(jnp.sum(coefficients[:BASIS, None, None] * matched, 0)) - coefficients[BASIS]
        wide_diff = jnp.pad(difference, ((FILT_HALF, FILT_HALF), (FILT_HALF, FILT_HALF)))
        filtered = along_rows_ref(along_cols_ref(wide_diff, smooth), smooth)[0]
        noise_power = lax.optimization_barrier(jnp.mean((difference * difference).reshape(ROWS, N_GRP, COLS), axis=(0, 2)))
        significance = filtered.reshape(ROWS, N_GRP, COLS) / jnp.sqrt(noise_power + epsilon)[None, :, None]
        return (difference, significance.reshape(ROWS, N_GRP * COLS), coefficients)
    differences, significances, coefficients = lax.map(exposure, (correlation, offset, science.reshape(N_VISIT, ROWS, N_GRP * COLS)))
    return (differences.reshape(strip_rows, N_GRP * COLS), significances.reshape(strip_rows, N_GRP * COLS), coefficients)
```

```python
import functools

import jax
import jax.numpy as jnp
import ml_dtypes
import numpy as np
from jax import lax
from jax.experimental import pallas as pl
from jax.experimental.pallas import tpu as pltpu
from jax.sharding import PartitionSpec as P

KER_HALF = 10
BASIS = 5
FILT_HALF = 6
RIDGE = 0.05
EPSILON = 1e-06

LANES = 128
PAIR = 2 * LANES
SHIFT = KER_HALF + FILT_HALF
MESH = pl.DeviceIdType.MESH

ROW_OF = (0, 1, 2, 3, 1)
COL_OF = (0, 1, 2, 1, 3)
N_COL = 4
N_SUMS = 26


def gauss(spread, half):
    points = np.arange(-half, half + 1, dtype=np.float64)
    return np.exp(-points * points / (2.0 * spread * spread))


def operator_taps():
    points = np.arange(-KER_HALF, KER_HALF + 1, dtype=np.float64)
    narrow, middle, wide = (gauss(s, KER_HALF) for s in (1.0, 1.8, 3.2))
    slope = points * middle / 1.8
    rows = (narrow, middle, wide, slope, middle)
    cols = (narrow, middle, wide, middle, slope)
    scales = [np.sqrt(np.sum(r * r) * np.sum(c * c)) for r, c in zip(rows, cols)]
    rows = [r / s for r, s in zip(rows, scales)]
    smooth = gauss(2.0, FILT_HALF)
    smooth = smooth / np.sqrt(np.sum(smooth * smooth))
    col_fields = (narrow, middle, wide, slope)
    return rows, col_fields, smooth


def banded(taps, n_out, n_in, shift):
    half = (len(taps) - 1) // 2
    gap = np.arange(n_in)[None, :] - np.arange(n_out)[:, None] - shift + half
    inside = (gap >= 0) & (gap < len(taps))
    return np.where(inside, taps[np.clip(gap, 0, len(taps) - 1)], 0.0)


def halves(x):
    x = x.astype(np.float32)
    high = x.astype(ml_dtypes.bfloat16)
    low = (x - high.astype(np.float32)).astype(ml_dtypes.bfloat16)
    return high, low


def row_stack(mats, depth):
    out = []
    for mat in mats:
        full = np.zeros((mat.shape[0], depth))
        full[:, : mat.shape[1]] = mat
        high, low = halves(full)
        out.append(np.concatenate([high, high, low], 1))
    return np.stack(out)


def constants(rows, cols, groups, depth):
    row_taps, col_taps, smooth = operator_taps()
    smooth_rows = banded(smooth, rows, rows, 0)
    span = rows + 2 * KER_HALF
    plain = [banded(r, rows, span, KER_HALF) for r in row_taps]
    row_ops = row_stack(plain + [smooth_rows @ m for m in plain], depth)
    smooth_op = row_stack([smooth_rows], rows)[0]

    def column_mats(keep_left, keep_right):
        wide = LANES + 2 * FILT_HALF
        keep = np.ones(wide)
        if not keep_left:
            keep[:FILT_HALF] = 0.0
        if not keep_right:
            keep[wide - FILT_HALF :] = 0.0
        gather = banded(smooth, LANES, wide, FILT_HALF) * keep[None, :]
        mats = [banded(c, LANES, PAIR, SHIFT) for c in col_taps]
        mats += [gather @ banded(c, wide, PAIR, SHIFT - FILT_HALF) for c in col_taps]
        return np.concatenate([m.T for m in mats], 1)

    def packed(mat):
        return np.stack(halves(mat))

    inner = packed(column_mats(True, True))
    left = packed(column_mats(False, True))
    right = packed(column_mats(True, False))
    col_ops = np.stack([inner, left, right])
    smooth_cols = packed(banded(smooth, LANES, PAIR, SHIFT).T)

    ones_rows = np.broadcast_to(smooth_rows.sum(1)[:, None], (rows, LANES))
    ones_cols = []
    for group in range(groups):
        columns = np.arange(cols)[:, None] + np.arange(-FILT_HALF, FILT_HALF + 1)[None, :]
        inside = (columns + group * cols >= 0) & (columns + group * cols < groups * cols)
        ones_cols.append(np.broadcast_to((inside * smooth).sum(1)[None], (8, cols)))
    return (
        row_ops,
        smooth_op,
        col_ops,
        smooth_cols,
        ones_rows.astype(np.float32),
        np.stack(ones_cols).astype(np.float32),
    )


def split(x):
    high = x.astype(jnp.bfloat16)
    low = (x - high.astype(jnp.float32)).astype(jnp.bfloat16)
    return high, low


def dot(a, b):
    return jnp.dot(a, b, preferred_element_type=jnp.float32)


def kernel(
    visits,
    groups,
    tiles_ref,
    science_ref,
    correlation_ref,
    offset_ref,
    row_ops_ref,
    smooth_op_ref,
    col_ops_ref,
    smooth_cols_ref,
    ones_rows_ref,
    ones_cols_ref,
    difference_ref,
    filtered_ref,
    small_ref,
    strip,
    outgoing,
    window,
    science,
    fields,
    stage,
    smoothed,
    sums,
    totals,
    place,
    places,
    row_ops,
    smooth_op,
    col_ops,
    smooth_cols,
    ones_rows,
    ones_cols,
    load_sems,
    place_send,
    place_recv,
    first_send,
    first_recv,
    second_send,
    second_recv,
    halo_send,
    halo_recv,
    total_send,
    total_recv,
):
    rows, cols = tiles_ref.shape
    blocks = cols // LANES
    pairs = blocks // 2
    chunks = blocks // visits
    half = visits // 2
    depth = window.shape[1]
    sent = outgoing.shape[2]
    me = lax.axis_index("visit")
    group = lax.axis_index("grp")
    has_left = group > 0
    has_right = group < groups - 1

    def block_of(chunk, owner):
        if chunk == 0:
            return owner + (owner // half) * (blocks - visits)
        return half + owner

    def lane(block):
        return pl.ds(pl.multiple_of(block * LANES, LANES), LANES)

    def other_visit(step):
        return lax.rem(me + step, visits)

    at_left = jnp.where(group == 0, 1, 0)
    at_right = jnp.where(group == groups - 1, 2, 0)
    loads = [
        (science_ref, science.at[:, pl.ds(LANES, cols)]),
        (smooth_op_ref, smooth_op),
        (smooth_cols_ref, smooth_cols),
        (row_ops_ref, row_ops),
        (col_ops_ref.at[0], col_ops.at[0]),
        (col_ops_ref.at[at_left], col_ops.at[1]),
        (col_ops_ref.at[at_right], col_ops.at[2]),
        (ones_rows_ref, ones_rows),
        (ones_cols_ref.at[group], ones_cols),
    ]
    for chunk in range(chunks):
        loads.append(
            (
                tiles_ref.at[:, lane(block_of(chunk, me))],
                strip[chunk].at[pl.ds(pl.multiple_of(me * rows, rows), rows), :],
            )
        )
    loads = [pltpu.make_async_copy(a, b, load_sems.at[i]) for i, (a, b) in enumerate(loads)]

    barrier = pltpu.get_barrier_semaphore()
    for step in range(1, visits):
        pl.semaphore_signal(
            barrier, inc=1, device_id=(other_visit(step), group), device_id_type=MESH
        )
    for step in range(1, groups):
        pl.semaphore_signal(
            barrier,
            inc=1,
            device_id=(me, lax.rem(group + step, groups)),
            device_id_type=MESH,
        )
    strip_rows = visits * rows
    first_row = correlation_ref[0] * rows + offset_ref[0] - KER_HALF
    first_row = lax.rem(first_row + strip_rows, strip_rows)
    place[...] = jnp.full(place.shape, first_row, jnp.int32)
    places[me] = jnp.full(place.shape, first_row, jnp.int32)
    window[:, sent:, :] = jnp.zeros((blocks + 2, depth - sent, LANES), jnp.float32)
    pl.semaphore_wait(barrier, visits - 1 + groups - 1)

    def place_copy(step, source=None):
        return pltpu.make_async_remote_copy(
            src_ref=place,
            dst_ref=places.at[me if source is None else source],
            send_sem=place_send.at[step],
            recv_sem=place_recv.at[me if source is None else source],
            device_id=(other_visit(step), group),
            device_id_type=MESH,
        )

    def first_copy(chunk, step, source=None):
        target = other_visit(step)
        source = me if source is None else source
        return pltpu.make_async_remote_copy(
            src_ref=tiles_ref.at[:, lane(block_of(chunk, target))],
            dst_ref=strip[chunk].at[pl.ds(pl.multiple_of(source * rows, rows), rows), :],
            send_sem=first_send.at[chunk, step],
            recv_sem=first_recv.at[chunk, source],
            device_id=(target, group),
            device_id_type=MESH,
        )

    def second_copy(chunk, step, source=None):
        target = other_visit(step)
        source = me if source is None else source
        return pltpu.make_async_remote_copy(
            src_ref=outgoing.at[chunk, target],
            dst_ref=window.at[block_of(chunk, source) + 1, pl.ds(0, sent), :],
            send_sem=second_send.at[chunk, step],
            recv_sem=second_recv.at[chunk, source],
            device_id=(target, group),
            device_id_type=MESH,
        )

    def halo_copy(index, source, target, neighbour):
        return pltpu.make_async_remote_copy(
            src_ref=source,
            dst_ref=target,
            send_sem=halo_send.at[index],
            recv_sem=halo_recv.at[index],
            device_id=(me, neighbour),
            device_id_type=MESH,
        )

    left = lax.rem(group + groups - 1, groups)
    right = lax.rem(group + 1, groups)
    last = blocks * LANES
    science_right = halo_copy(
        0, science_ref.at[:, pl.ds(last - LANES, LANES)], science.at[:, pl.ds(0, LANES)], right
    )
    science_left = halo_copy(
        1, science_ref.at[:, pl.ds(0, LANES)], science.at[:, pl.ds(last + LANES, LANES)], left
    )
    window_right = halo_copy(
        2, window.at[blocks, pl.ds(0, sent), :], window.at[0, pl.ds(0, sent), :], right
    )
    window_left = halo_copy(
        3, window.at[1, pl.ds(0, sent), :], window.at[blocks + 1, pl.ds(0, sent), :], left
    )

    for step in range(1, visits):
        place_copy(step).start()
    for chunk in range(chunks):
        for step in range(1, visits):
            first_copy(chunk, step).start()

    @pl.when(has_right)
    def _():
        science_right.start()

    @pl.when(has_left)
    def _():
        science_left.start()

    for load in loads:
        load.start()

    @pl.when(jnp.logical_not(has_left))
    def _():
        science[:, 0:LANES] = jnp.zeros((rows, LANES), jnp.float32)
        window[0, 0:sent, :] = jnp.zeros((sent, LANES), jnp.float32)

    @pl.when(jnp.logical_not(has_right))
    def _():
        science[:, last + LANES :] = jnp.zeros((rows, LANES), jnp.float32)
        window[blocks + 1, 0:sent, :] = jnp.zeros((sent, LANES), jnp.float32)

    sums[...] = jnp.zeros(sums.shape, jnp.float32)
    for load in loads:
        load.wait()

    @pl.when(has_left)
    def _():
        science_right.wait_recv()

    @pl.when(has_right)
    def _():
        science_left.wait_recv()

    def science_pair(pair, carry):
        four = science[:, pl.ds(pl.multiple_of(pair * PAIR, PAIR), 2 * PAIR)]
        four = pltpu.roll(four, 2 * PAIR - (LANES - SHIFT), 1)
        high, low = split(four)
        for j in range(2):
            at = slice(j * LANES, j * LANES + PAIR)
            field = (
                dot(high[:, at], smooth_cols[0])
                + dot(low[:, at], smooth_cols[0])
                + dot(high[:, at], smooth_cols[1])
            )
            h, l = split(field)
            out = slice(j * LANES, (j + 1) * LANES)
            stage[0, 0:rows, out] = h
            stage[0, rows : 2 * rows, out] = l
            stage[0, 2 * rows : 3 * rows, out] = h
        smoothed[pair] = dot(smooth_op[...], stage[0, 0 : 3 * rows, :])
        return carry

    lax.fori_loop(0, pairs, science_pair, 0)

    for step in range(1, visits):
        place_copy(step, other_visit(step)).wait_recv()
    for chunk in range(chunks):
        for step in range(1, visits):
            first_copy(chunk, step, other_visit(step)).wait_recv()
        end = visits * rows
        extra = strip[chunk].shape[0] - end
        strip[chunk][end:, :] = strip[chunk][0:extra, :]

        def cut(step, carry):
            target = lax.rem(me + step, visits)
            start = places[target][0, 0]
            outgoing[chunk, target] = strip[chunk][pl.ds(start, sent), :]
            return carry

        for step in range(1, visits):
            cut(step, 0)
            second_copy(chunk, step).start()
        window[block_of(chunk, me) + 1, 0:sent, :] = strip[chunk][
            pl.ds(places[me][0, 0], sent), :
        ]

    def wait_block(chunk, owner):
        @pl.when(owner != me)
        def _():
            second_copy(chunk, 1, owner).wait_recv()

    in_left = me < half

    def exposure_pair(index, carry):
        @pl.when(index == 0)
        def _():
            wait_block(0, 0)
            wait_block(0, visits - 1)

            @pl.when(has_right)
            def _():
                window_right.start()

            @pl.when(has_left)
            def _():
                window_left.start()

            for owner in range(1, visits - 1):
                wait_block(0, owner)
            if chunks != 2:
                for chunk in range(1, chunks):
                    for owner in range(visits):
                        wait_block(chunk, owner)

            @pl.when(has_left)
            def _():
                window_right.wait_recv()

            @pl.when(has_right)
            def _():
                window_left.wait_recv()

        pair = jnp.where(index == 0, 0, jnp.where(index == 1, pairs - 1, index - 1))
        pair = jnp.where(in_left, pair, pairs - 1 - pair)

        if chunks == 2:
            done = 0
            for at in range(2, pairs):
                upto = min(visits, max(done, 2 * (at - 1) + 3 - half))
                if upto > done:

                    @pl.when(index == at)
                    def _(done=done, upto=upto):
                        for k in range(done, upto):
                            wait_block(1, jnp.where(in_left, k, visits - 1 - k))

                done = upto

        four = jnp.concatenate([window[2 * pair + k] for k in range(4)], 1)
        four = pltpu.roll(four, 2 * PAIR - (LANES - SHIFT), 1)
        high, low = split(four)
        for j in range(2):
            at = slice(j * LANES, j * LANES + PAIR)
            if j == 0:
                which = jnp.where(pair == 0, 1, 0)
            else:
                which = jnp.where(pair == pairs - 1, 2, 0)
            field = (
                dot(high[:, at], col_ops[which, 0])
                + dot(low[:, at], col_ops[which, 0])
                + dot(high[:, at], col_ops[which, 1])
            )
            out = slice(j * LANES, (j + 1) * LANES)
            for f in range(2 * N_COL):
                h, l = split(field[:, f * LANES : (f + 1) * LANES])
                stage[f, 0:depth, out] = h
                stage[f, depth : 2 * depth, out] = l
                stage[f, 2 * depth : 3 * depth, out] = h
        for b in range(BASIS):
            fields[pair, b] = dot(row_ops[b], stage[COL_OF[b]])
            fields[pair, BASIS + b] = dot(row_ops[BASIS + b], stage[N_COL + COL_OF[b]])

        def gather(slab, acc):
            at = pl.ds(pl.multiple_of(slab * 8, 8), 8)
            acc = list(acc)
            for j in range(2):
                cut_at = slice(j * LANES, (j + 1) * LANES)
                m = [fields[pair, b, at, cut_at] for b in range(BASIS)]
                lanes = pl.ds(pl.multiple_of(pair * PAIR + (j + 1) * LANES, LANES), LANES)
                s = science[at, lanes]
                terms = [m[b] * m[c] for b in range(BASIS) for c in range(b, BASIS)]
                terms += m + [m[b] * s for b in range(BASIS)] + [s]
                acc = [a + t for a, t in zip(acc, terms)]
            return tuple(acc)

        acc = tuple(sums[k] for k in range(N_SUMS))
        acc = lax.fori_loop(0, rows // 8, gather, acc, unroll=2)
        for k in range(N_SUMS):
            sums[k] = acc[k]
        return carry

    lax.fori_loop(0, pairs, exposure_pair, 0)

    totals[group] = jnp.sum(sums[...], axis=1)

    def total_copy(step, source=None):
        source = group if source is None else source
        return pltpu.make_async_remote_copy(
            src_ref=totals.at[source],
            dst_ref=totals.at[source],
            send_sem=total_send.at[step],
            recv_sem=total_recv.at[source],
            device_id=(me, lax.rem(group + step, groups)),
            device_id_type=MESH,
        )

    for step in range(1, groups):
        total_copy(step).start()
    for step in range(1, groups):
        total_copy(step, lax.rem(group + step, groups)).wait_recv()
    total = totals[0]
    for g in range(1, groups):
        total = total + totals[g]
    counted = float(rows * cols * groups)
    total = jnp.sum(total, axis=1, keepdims=True) / counted
    entry = [jnp.broadcast_to(total[k : k + 1, :], (8, LANES)) for k in range(N_SUMS)]

    size = BASIS + 1
    normal = {}
    at = 0
    for b in range(BASIS):
        for c in range(b, BASIS):
            normal[b, c] = entry[at] + RIDGE if b == c else entry[at]
            at += 1
    for b in range(BASIS):
        normal[b, BASIS] = entry[at + b]
    normal[BASIS, BASIS] = jnp.full((8, LANES), 1.0 + RIDGE, jnp.float32)
    rhs = [entry[at + BASIS + b] for b in range(size)]
    inverse = []
    for k in range(size):
        inverse.append(1.0 / normal[k, k])
        for i in range(k + 1, size):
            factor = normal[k, i] * inverse[k]
            for j in range(i, size):
                normal[i, j] = normal[i, j] - factor * normal[k, j]
            rhs[i] = rhs[i] - factor * rhs[k]
    coef = [None] * size
    for k in reversed(range(size)):
        value = rhs[k]
        for j in range(k + 1, size):
            value = value - normal[k, j] * coef[j]
        coef[k] = value * inverse[k]

    def combine(slab, power):
        at = pl.ds(pl.multiple_of(slab * 8, 8), 8)
        edge = coef[BASIS] * ones_rows[at, :]
        for pair in range(pairs):
            for j in range(2):
                cut_at = slice(j * LANES, (j + 1) * LANES)
                first = pair * PAIR + j * LANES
                s = science[at, first + LANES : first + 2 * LANES]
                f = smoothed[pair, at, cut_at] - edge * ones_cols[:, first : first + LANES]
                m = coef[0] * fields[pair, 0, at, cut_at]
                g = coef[0] * fields[pair, BASIS, at, cut_at]
                for b in range(1, BASIS):
                    m = m + coef[b] * fields[pair, b, at, cut_at]
                    g = g + coef[b] * fields[pair, BASIS + b, at, cut_at]
                partial = s - m
                difference_ref[at, first : first + LANES] = partial
                filtered_ref[at, first : first + LANES] = f - g
                whole = partial - coef[BASIS]
                power = power + whole * whole
        return power

    power = lax.fori_loop(0, rows // 8, combine, jnp.zeros((8, LANES), jnp.float32))
    power = jnp.sum(jnp.sum(power, axis=1, keepdims=True), axis=0, keepdims=True)
    scale = 1.0 / jnp.sqrt(power / float(rows * cols) + EPSILON)
    column = lax.broadcasted_iota(jnp.int32, (8, LANES), 1)
    small = jnp.broadcast_to(scale, (8, LANES))
    for k in range(size):
        small = jnp.where(column == k, coef[k], small)
    small_ref[...] = small

    for step in range(1, visits):
        place_copy(step).wait_send()
        for chunk in range(chunks):
            first_copy(chunk, step).wait_send()
            second_copy(chunk, step).wait_send()
    for step in range(1, groups):
        total_copy(step).wait_send()

    @pl.when(has_right)
    def _():
        science_right.wait_send()
        window_right.wait_send()

    @pl.when(has_left)
    def _():
        science_left.wait_send()
        window_left.wait_send()


def shards(coadd_tiles, science, correlation, offset):
    visits = lax.axis_size("visit")
    groups = lax.axis_size("grp")
    rows, cols = coadd_tiles.shape
    blocks = cols // LANES
    pairs = blocks // 2
    chunks = blocks // visits
    span = rows + 2 * KER_HALF
    sent = -(-span // 8) * 8
    depth = -(-span // 16) * 16
    consts = constants(rows, cols, groups, depth)
    row_ops, smooth_op, col_ops, smooth_cols, ones_rows, ones_cols = consts
    f32, bf16 = jnp.float32, jnp.bfloat16
    anywhere = pl.BlockSpec(memory_space=pl.ANY)
    scalar = pl.BlockSpec(memory_space=pltpu.SMEM)
    vmem = pl.BlockSpec(memory_space=pltpu.VMEM)
    dma = pltpu.SemaphoreType.DMA
    difference, filtered, small = pl.pallas_call(
        functools.partial(kernel, visits, groups),
        out_shape=(
            jax.ShapeDtypeStruct((rows, cols), f32),
            jax.ShapeDtypeStruct((rows, cols), f32),
            jax.ShapeDtypeStruct((8, LANES), f32),
        ),
        in_specs=[anywhere, anywhere, scalar, scalar] + [anywhere] * 6,
        out_specs=(vmem, vmem, vmem),
        scratch_shapes=[
            (pltpu.VMEM((visits * rows + sent, LANES), f32),) * chunks,
            pltpu.VMEM((chunks, visits, sent, LANES), f32),
            pltpu.VMEM((blocks + 2, depth, LANES), f32),
            pltpu.VMEM((rows, cols + 2 * LANES), f32),
            pltpu.VMEM((pairs, 2 * BASIS, rows, PAIR), f32),
            pltpu.VMEM((2 * N_COL, 3 * depth, PAIR), bf16),
            pltpu.VMEM((pairs, rows, PAIR), f32),
            pltpu.VMEM((32, 8, LANES), f32),
            pltpu.VMEM((groups, 32, LANES), f32),
            pltpu.VMEM((8, LANES), jnp.int32),
            pltpu.VMEM((visits, 8, LANES), jnp.int32),
            pltpu.VMEM(row_ops.shape, bf16),
            pltpu.VMEM(smooth_op.shape, bf16),
            pltpu.VMEM(col_ops.shape, bf16),
            pltpu.VMEM(smooth_cols.shape, bf16),
            pltpu.VMEM(ones_rows.shape, f32),
            pltpu.VMEM(ones_cols.shape[1:], f32),
            dma((9 + chunks,)),
            dma((visits,)),
            dma((visits,)),
            dma((chunks, visits)),
            dma((chunks, visits)),
            dma((chunks, visits)),
            dma((chunks, visits)),
            dma((4,)),
            dma((4,)),
            dma((groups,)),
            dma((groups,)),
        ],
        compiler_params=pltpu.CompilerParams(
            collective_id=0, has_side_effects=True, vmem_limit_bytes=60 * 1024 * 1024
        ),
        name="difference_imaging",
    )(coadd_tiles, science, correlation, offset, *[jnp.asarray(c) for c in consts])
    coefficients = small[0:1, : BASIS + 1]
    return (
        difference - small[0, BASIS],
        filtered * small[0, BASIS + 1],
        coefficients,
    )


def solution(mesh):
    in_specs = (P("visit", "grp"), P("visit", "grp"), P("visit"), P("visit"))
    out_specs = (P("visit", "grp"), P("visit", "grp"), P("visit", None))
    return jax.shard_map(shards, mesh=mesh, in_specs=in_specs, out_specs=out_specs, check_vma=False)
```

```python
import functools

import jax
import jax.numpy as jnp
import ml_dtypes
import numpy as np
from jax import lax
from jax.experimental import pallas as pl
from jax.experimental.pallas import tpu as pltpu
from jax.sharding import PartitionSpec as P

KER_HALF = 10
BASIS = 5
FILT_HALF = 6
RIDGE = 0.05
EPSILON = 1e-06

LANES = 128
PAIR = 2 * LANES
SHIFT = KER_HALF + FILT_HALF
MESH = pl.DeviceIdType.MESH

ROW_OF = (0, 1, 2, 3, 1)
COL_OF = (0, 1, 2, 1, 3)
N_COL = 4
N_SUMS = 26
PARTS = 4


def gauss(spread, half):
    points = np.arange(-half, half + 1, dtype=np.float64)
    return np.exp(-points * points / (2.0 * spread * spread))


def operator_taps():
    points = np.arange(-KER_HALF, KER_HALF + 1, dtype=np.float64)
    narrow, middle, wide = (gauss(s, KER_HALF) for s in (1.0, 1.8, 3.2))
    slope = points * middle / 1.8
    rows = (narrow, middle, wide, slope, middle)
    cols = (narrow, middle, wide, middle, slope)
    scales = [np.sqrt(np.sum(r * r) * np.sum(c * c)) for r, c in zip(rows, cols)]
    rows = [r / s for r, s in zip(rows, scales)]
    smooth = gauss(2.0, FILT_HALF)
    smooth = smooth / np.sqrt(np.sum(smooth * smooth))
    col_fields = (narrow, middle, wide, slope)
    return rows, col_fields, smooth


def banded(taps, n_out, n_in, shift):
    half = (len(taps) - 1) // 2
    gap = np.arange(n_in)[None, :] - np.arange(n_out)[:, None] - shift + half
    inside = (gap >= 0) & (gap < len(taps))
    return np.where(inside, taps[np.clip(gap, 0, len(taps) - 1)], 0.0)


def halves(x):
    x = x.astype(np.float32)
    high = x.astype(ml_dtypes.bfloat16)
    low = (x - high.astype(np.float32)).astype(ml_dtypes.bfloat16)
    return high, low


def row_stack(mats, depth):
    out = []
    for mat in mats:
        full = np.zeros((mat.shape[0], depth))
        full[:, : mat.shape[1]] = mat
        high, low = halves(full)
        out.append(np.concatenate([high, high, low], 1))
    return np.stack(out)


def lower_start(rows):
    return rows // 2 - 8


def halved_rows(mats, rows, reach):
    upper = row_stack([m[: rows // 2, :reach] for m in mats], reach)
    low = lower_start(rows)
    lower = row_stack([m[rows // 2 :, low : low + reach] for m in mats], reach)
    return np.stack([upper, lower])


def constants(rows, cols, groups, reach):
    row_taps, col_taps, smooth = operator_taps()
    smooth_rows = banded(smooth, rows, rows, 0)
    span = rows + 2 * KER_HALF
    plain = [banded(r, rows, span, KER_HALF) for r in row_taps]
    row_ops = halved_rows(plain + [smooth_rows @ m for m in plain], rows, reach)
    smooth_op = row_stack([smooth_rows], rows)[0]

    def column_mats(keep_left, keep_right):
        wide = LANES + 2 * FILT_HALF
        keep = np.ones(wide)
        if not keep_left:
            keep[:FILT_HALF] = 0.0
        if not keep_right:
            keep[wide - FILT_HALF :] = 0.0
        gather = banded(smooth, LANES, wide, FILT_HALF) * keep[None, :]
        mats = [banded(c, LANES, PAIR, SHIFT) for c in col_taps]
        mats += [gather @ banded(c, wide, PAIR, SHIFT - FILT_HALF) for c in col_taps]
        return np.concatenate([m.T for m in mats], 1)

    def packed(mat):
        return np.stack(halves(mat))

    inner = packed(column_mats(True, True))
    left = packed(column_mats(False, True))
    right = packed(column_mats(True, False))
    col_ops = np.stack([inner, left, right])
    smooth_cols = packed(banded(smooth, LANES, PAIR, SHIFT).T)

    ones_rows = np.broadcast_to(smooth_rows.sum(1)[:, None], (rows, LANES))
    ones_cols = []
    for group in range(groups):
        columns = np.arange(cols)[:, None] + np.arange(-FILT_HALF, FILT_HALF + 1)[None, :]
        inside = (columns + group * cols >= 0) & (columns + group * cols < groups * cols)
        ones_cols.append(np.broadcast_to((inside * smooth).sum(1)[None], (8, cols)))
    return (
        row_ops,
        smooth_op,
        col_ops,
        smooth_cols,
        ones_rows.astype(np.float32),
        np.stack(ones_cols).astype(np.float32),
    )


def split(x):
    high = x.astype(jnp.bfloat16)
    low = (x - high.astype(jnp.float32)).astype(jnp.bfloat16)
    return high, low


def dot(a, b):
    return jnp.dot(a, b, preferred_element_type=jnp.float32)


def kernel(
    visits,
    groups,
    tiles_ref,
    science_ref,
    correlation_ref,
    offset_ref,
    row_ops_ref,
    smooth_op_ref,
    col_ops_ref,
    smooth_cols_ref,
    ones_rows_ref,
    ones_cols_ref,
    difference_ref,
    filtered_ref,
    small_ref,
    strip,
    outgoing,
    window,
    science,
    fields,
    stage,
    smooth_stage,
    smoothed,
    sums,
    totals,
    place,
    places,
    row_ops,
    smooth_op,
    col_ops,
    smooth_cols,
    ones_rows,
    ones_cols,
    load_sems,
    place_send,
    place_recv,
    first_send,
    first_recv,
    second_send,
    second_recv,
    halo_send,
    halo_recv,
    total_send,
    total_recv,
):
    rows, cols = tiles_ref.shape
    blocks = cols // LANES
    pairs = blocks // 2
    chunks = blocks // visits
    half = visits // 2
    depth = window.shape[1]
    sent = outgoing.shape[2]
    reach = sent - lower_start(rows)
    me = lax.axis_index("visit")
    group = lax.axis_index("grp")
    has_left = group > 0
    has_right = group < groups - 1

    def block_of(chunk, owner):
        if chunk == 0:
            return owner + (owner // half) * (blocks - visits)
        return half + owner

    def lane(block):
        return pl.ds(pl.multiple_of(block * LANES, LANES), LANES)

    def other_visit(step):
        return lax.rem(me + step, visits)

    at_left = jnp.where(group == 0, 1, 0)
    at_right = jnp.where(group == groups - 1, 2, 0)
    loads = [
        (science_ref, science.at[:, pl.ds(LANES, cols)]),
        (smooth_op_ref, smooth_op),
        (smooth_cols_ref, smooth_cols),
        (row_ops_ref, row_ops),
        (col_ops_ref.at[0], col_ops.at[0]),
        (col_ops_ref.at[at_left], col_ops.at[1]),
        (col_ops_ref.at[at_right], col_ops.at[2]),
        (ones_rows_ref, ones_rows),
        (ones_cols_ref.at[group], ones_cols),
    ]
    for chunk in range(chunks):
        loads.append(
            (
                tiles_ref.at[:, lane(block_of(chunk, me))],
                strip[chunk].at[pl.ds(pl.multiple_of(me * rows, rows), rows), :],
            )
        )
    loads = [pltpu.make_async_copy(a, b, load_sems.at[i]) for i, (a, b) in enumerate(loads)]

    barrier = pltpu.get_barrier_semaphore()
    for step in range(1, visits):
        pl.semaphore_signal(
            barrier, inc=1, device_id=(other_visit(step), group), device_id_type=MESH
        )
    for step in range(1, groups):
        pl.semaphore_signal(
            barrier,
            inc=1,
            device_id=(me, lax.rem(group + step, groups)),
            device_id_type=MESH,
        )
    strip_rows = visits * rows
    first_row = correlation_ref[0] * rows + offset_ref[0] - KER_HALF
    first_row = lax.rem(first_row + strip_rows, strip_rows)
    place[...] = jnp.full(place.shape, first_row, jnp.int32)
    places[me] = jnp.full(place.shape, first_row, jnp.int32)
    window[:, sent:, :] = jnp.zeros((blocks + 2, depth - sent, LANES), jnp.float32)
    pl.semaphore_wait(barrier, visits - 1 + groups - 1)

    def place_copy(step, source=None):
        return pltpu.make_async_remote_copy(
            src_ref=place,
            dst_ref=places.at[me if source is None else source],
            send_sem=place_send.at[step],
            recv_sem=place_recv.at[me if source is None else source],
            device_id=(other_visit(step), group),
            device_id_type=MESH,
        )

    def first_copy(chunk, step, source=None):
        target = other_visit(step)
        source = me if source is None else source
        return pltpu.make_async_remote_copy(
            src_ref=tiles_ref.at[:, lane(block_of(chunk, target))],
            dst_ref=strip[chunk].at[pl.ds(pl.multiple_of(source * rows, rows), rows), :],
            send_sem=first_send.at[chunk, step],
            recv_sem=first_recv.at[chunk, source],
            device_id=(target, group),
            device_id_type=MESH,
        )

    def second_copy(chunk, step, source=None):
        target = other_visit(step)
        source = me if source is None else source
        return pltpu.make_async_remote_copy(
            src_ref=outgoing.at[chunk, target],
            dst_ref=window.at[block_of(chunk, source) + 1, pl.ds(0, sent), :],
            send_sem=second_send.at[chunk, step],
            recv_sem=second_recv.at[chunk, source],
            device_id=(target, group),
            device_id_type=MESH,
        )

    def halo_copy(index, source, target, neighbour):
        return pltpu.make_async_remote_copy(
            src_ref=source,
            dst_ref=target,
            send_sem=halo_send.at[index],
            recv_sem=halo_recv.at[index],
            device_id=(me, neighbour),
            device_id_type=MESH,
        )

    left = lax.rem(group + groups - 1, groups)
    right = lax.rem(group + 1, groups)
    last = blocks * LANES
    science_right = halo_copy(
        0, science_ref.at[:, pl.ds(last - LANES, LANES)], science.at[:, pl.ds(0, LANES)], right
    )
    science_left = halo_copy(
        1, science_ref.at[:, pl.ds(0, LANES)], science.at[:, pl.ds(last + LANES, LANES)], left
    )
    window_right = halo_copy(
        2, window.at[blocks, pl.ds(0, sent), :], window.at[0, pl.ds(0, sent), :], right
    )
    window_left = halo_copy(
        3, window.at[1, pl.ds(0, sent), :], window.at[blocks + 1, pl.ds(0, sent), :], left
    )

    for step in range(1, visits):
        place_copy(step).start()
    for chunk in range(chunks):
        for step in range(1, visits):
            first_copy(chunk, step).start()

    @pl.when(has_right)
    def _():
        science_right.start()

    @pl.when(has_left)
    def _():
        science_left.start()

    for load in loads:
        load.start()

    @pl.when(jnp.logical_not(has_left))
    def _():
        science[:, 0:LANES] = jnp.zeros((rows, LANES), jnp.float32)
        window[0, 0:sent, :] = jnp.zeros((sent, LANES), jnp.float32)

    @pl.when(jnp.logical_not(has_right))
    def _():
        science[:, last + LANES :] = jnp.zeros((rows, LANES), jnp.float32)
        window[blocks + 1, 0:sent, :] = jnp.zeros((sent, LANES), jnp.float32)

    sums[...] = jnp.zeros(sums.shape, jnp.float32)
    for load in loads:
        load.wait()

    @pl.when(has_left)
    def _():
        science_right.wait_recv()

    @pl.when(has_right)
    def _():
        science_left.wait_recv()

    def science_pair(pair, carry):
        four = science[:, pl.ds(pl.multiple_of(pair * PAIR, PAIR), 2 * PAIR)]
        four = pltpu.roll(four, 2 * PAIR - (LANES - SHIFT), 1)
        high, low = split(four)
        for j in range(2):
            at = slice(j * LANES, j * LANES + PAIR)
            field = (
                dot(high[:, at], smooth_cols[0])
                + dot(low[:, at], smooth_cols[0])
                + dot(high[:, at], smooth_cols[1])
            )
            h, l = split(field)
            out = slice(j * LANES, (j + 1) * LANES)
            smooth_stage[0:rows, out] = h
            smooth_stage[rows : 2 * rows, out] = l
            smooth_stage[2 * rows : 3 * rows, out] = h
        smoothed[pair] = dot(smooth_op[...], smooth_stage[...])
        return carry

    lax.fori_loop(0, pairs, science_pair, 0)

    for step in range(1, visits):
        place_copy(step, other_visit(step)).wait_recv()
    for chunk in range(chunks):
        for step in range(1, visits):
            first_copy(chunk, step, other_visit(step)).wait_recv()
        end = visits * rows
        extra = strip[chunk].shape[0] - end
        strip[chunk][end:, :] = strip[chunk][0:extra, :]

        def cut(step, carry):
            target = lax.rem(me + step, visits)
            start = places[target][0, 0]
            outgoing[chunk, target] = strip[chunk][pl.ds(start, sent), :]
            return carry

        for step in range(1, visits):
            cut(step, 0)
            second_copy(chunk, step).start()
        window[block_of(chunk, me) + 1, 0:sent, :] = strip[chunk][
            pl.ds(places[me][0, 0], sent), :
        ]

    def wait_block(chunk, owner):
        @pl.when(owner != me)
        def _():
            second_copy(chunk, 1, owner).wait_recv()

    in_left = me < half

    def exposure_pair(index, carry):
        @pl.when(index == 0)
        def _():
            wait_block(0, 0)
            wait_block(0, visits - 1)

            @pl.when(has_right)
            def _():
                window_right.start()

            @pl.when(has_left)
            def _():
                window_left.start()

            for owner in range(1, visits - 1):
                wait_block(0, owner)
            if chunks != 2:
                for chunk in range(1, chunks):
                    for owner in range(visits):
                        wait_block(chunk, owner)

            @pl.when(has_left)
            def _():
                window_right.wait_recv()

            @pl.when(has_right)
            def _():
                window_left.wait_recv()

        pair = jnp.where(index == 0, 0, jnp.where(index == 1, pairs - 1, index - 1))
        pair = jnp.where(in_left, pair, pairs - 1 - pair)

        if chunks == 2:
            done = 0
            for at in range(2, pairs):
                upto = min(visits, max(done, 2 * (at - 1) + 3 - half))
                if upto > done:

                    @pl.when(index == at)
                    def _(done=done, upto=upto):
                        for k in range(done, upto):
                            wait_block(1, jnp.where(in_left, k, visits - 1 - k))

                done = upto

        four = jnp.concatenate([window[2 * pair + k] for k in range(4)], 1)
        four = pltpu.roll(four, 2 * PAIR - (LANES - SHIFT), 1)
        high, low = split(four)
        for j in range(2):
            at = slice(j * LANES, j * LANES + PAIR)
            if j == 0:
                which = jnp.where(pair == 0, 1, 0)
            else:
                which = jnp.where(pair == pairs - 1, 2, 0)
            field = (
                dot(high[:, at], col_ops[which, 0])
                + dot(low[:, at], col_ops[which, 0])
                + dot(high[:, at], col_ops[which, 1])
            )
            out = slice(j * LANES, (j + 1) * LANES)
            for f in range(2 * N_COL):
                for part in range(2):
                    first = part * lower_start(rows)
                    h, l = split(field[first : first + reach, f * LANES : (f + 1) * LANES])
                    stage[f, part, 0:reach, out] = h
                    stage[f, part, reach : 2 * reach, out] = l
                    stage[f, part, 2 * reach : 3 * reach, out] = h
        for part in range(2):
            into = slice(part * (rows // 2), (part + 1) * (rows // 2))
            for b in range(BASIS):
                for at, f in ((b, COL_OF[b]), (BASIS + b, N_COL + COL_OF[b])):
                    fields[pair, at, into, :] = dot(row_ops[part, at], stage[f, part])

        def gather(slab, acc):
            at = pl.ds(pl.multiple_of(slab * 8, 8), 8)
            acc = list(acc)
            for j in range(2):
                cut_at = slice(j * LANES, (j + 1) * LANES)
                m = [fields[pair, b, at, cut_at] for b in range(BASIS)]
                lanes = pl.ds(pl.multiple_of(pair * PAIR + (j + 1) * LANES, LANES), LANES)
                s = science[at, lanes]
                terms = [m[b] * m[c] for b in range(BASIS) for c in range(b, BASIS)]
                terms += m + [m[b] * s for b in range(BASIS)] + [s]
                acc = [a + t for a, t in zip(acc, terms)]
            return tuple(acc)

        acc = tuple(sums[k] for k in range(N_SUMS))
        acc = lax.fori_loop(0, rows // 8, gather, acc, unroll=2)
        for k in range(N_SUMS):
            sums[k] = acc[k]
        return carry

    lax.fori_loop(0, pairs, exposure_pair, 0)

    totals[group] = jnp.sum(sums[...], axis=1)

    def total_copy(step, source=None):
        source = group if source is None else source
        return pltpu.make_async_remote_copy(
            src_ref=totals.at[source],
            dst_ref=totals.at[source],
            send_sem=total_send.at[step],
            recv_sem=total_recv.at[source],
            device_id=(me, lax.rem(group + step, groups)),
            device_id_type=MESH,
        )

    for step in range(1, groups):
        total_copy(step).start()
    for step in range(1, groups):
        total_copy(step, lax.rem(group + step, groups)).wait_recv()
    total = totals[0]
    for g in range(1, groups):
        total = total + totals[g]
    counted = float(rows * cols * groups)
    total = jnp.sum(total, axis=1, keepdims=True) / counted
    entry = [jnp.broadcast_to(total[k : k + 1, :], (8, LANES)) for k in range(N_SUMS)]

    size = BASIS + 1
    normal = {}
    at = 0
    for b in range(BASIS):
        for c in range(b, BASIS):
            normal[b, c] = entry[at] + RIDGE if b == c else entry[at]
            at += 1
    for b in range(BASIS):
        normal[b, BASIS] = entry[at + b]
    normal[BASIS, BASIS] = jnp.full((8, LANES), 1.0 + RIDGE, jnp.float32)
    rhs = [entry[at + BASIS + b] for b in range(size)]
    inverse = []
    for k in range(size):
        inverse.append(1.0 / normal[k, k])
        for i in range(k + 1, size):
            factor = normal[k, i] * inverse[k]
            for j in range(i, size):
                normal[i, j] = normal[i, j] - factor * normal[k, j]
            rhs[i] = rhs[i] - factor * rhs[k]
    coef = [None] * size
    for k in reversed(range(size)):
        value = rhs[k]
        for j in range(k + 1, size):
            value = value - normal[k, j] * coef[j]
        coef[k] = value * inverse[k]

    def combine(slab, power):
        at = pl.ds(pl.multiple_of(slab * 8, 8), 8)
        edge = coef[BASIS] * ones_rows[at, :]
        for pair in range(pairs):
            for j in range(2):
                cut_at = slice(j * LANES, (j + 1) * LANES)
                first = pair * PAIR + j * LANES
                s = science[at, first + LANES : first + 2 * LANES]
                f = smoothed[pair, at, cut_at] - edge * ones_cols[:, first : first + LANES]
                m = coef[0] * fields[pair, 0, at, cut_at]
                g = coef[0] * fields[pair, BASIS, at, cut_at]
                for b in range(1, BASIS):
                    m = m + coef[b] * fields[pair, b, at, cut_at]
                    g = g + coef[b] * fields[pair, BASIS + b, at, cut_at]
                partial = s - m
                whole = partial - coef[BASIS]
                difference_ref[at, first : first + LANES] = whole
                filtered_ref[at, first : first + LANES] = f - g
                power = power + whole * whole
        return power

    power = lax.fori_loop(0, rows // 8, combine, jnp.zeros((8, LANES), jnp.float32))
    power = jnp.sum(jnp.sum(power, axis=1, keepdims=True), axis=0, keepdims=True)
    scale = 1.0 / jnp.sqrt(power / float(rows * cols) + EPSILON)
    column = lax.broadcasted_iota(jnp.int32, (8, LANES), 1)
    row = lax.broadcasted_iota(jnp.int32, (8, LANES), 0)
    small = jnp.broadcast_to(scale, (8, LANES))
    for k in range(size):
        small = jnp.where((row == 0) & (column == k), coef[k], small)
    small_ref[...] = small

    for step in range(1, visits):
        place_copy(step).wait_send()
        for chunk in range(chunks):
            first_copy(chunk, step).wait_send()
            second_copy(chunk, step).wait_send()
    for step in range(1, groups):
        total_copy(step).wait_send()

    @pl.when(has_right)
    def _():
        science_right.wait_send()
        window_right.wait_send()

    @pl.when(has_left)
    def _():
        science_left.wait_send()
        window_left.wait_send()


def finish(difference, filtered, small, difference_ref, significance_ref, coef_ref, scaled, sems, sem):
    out = pltpu.make_async_copy(difference, difference_ref, sem)
    out.start()
    scale = small[1:2, 0:1]
    size = difference.shape[0] // PARTS
    copies = []
    for part in range(PARTS):
        at = pl.ds(part * size, size)
        scaled[part] = filtered[at, :] * scale
        copies.append(
            pltpu.make_async_copy(scaled.at[part], significance_ref.at[at, :], sems.at[part])
        )
        copies[-1].start()
    coef_ref[...] = small[0:1, 0 : BASIS + 1]
    out.wait()
    for copy in copies:
        copy.wait()


def shards(coadd_tiles, science, correlation, offset):
    visits = lax.axis_size("visit")
    groups = lax.axis_size("grp")
    rows, cols = coadd_tiles.shape
    blocks = cols // LANES
    pairs = blocks // 2
    chunks = blocks // visits
    span = rows + 2 * KER_HALF
    sent = -(-span // 8) * 8
    depth = -(-span // 16) * 16
    reach = sent - lower_start(rows)
    consts = constants(rows, cols, groups, reach)
    row_ops, smooth_op, col_ops, smooth_cols, ones_rows, ones_cols = consts
    f32, bf16 = jnp.float32, jnp.bfloat16
    anywhere = pl.BlockSpec(memory_space=pl.ANY)
    scalar = pl.BlockSpec(memory_space=pltpu.SMEM)
    vmem = pl.BlockSpec(memory_space=pltpu.VMEM)
    dma = pltpu.SemaphoreType.DMA
    difference, filtered, small = pl.pallas_call(
        functools.partial(kernel, visits, groups),
        out_shape=(
            pltpu.VMEM((rows, cols), f32),
            pltpu.VMEM((rows, cols), f32),
            pltpu.VMEM((8, LANES), f32),
        ),
        in_specs=[anywhere, anywhere, scalar, scalar] + [anywhere] * 6,
        out_specs=(vmem, vmem, vmem),
        scratch_shapes=[
            (pltpu.VMEM((visits * rows + sent, LANES), f32),) * chunks,
            pltpu.VMEM((chunks, visits, sent, LANES), f32),
            pltpu.VMEM((blocks + 2, depth, LANES), f32),
            pltpu.VMEM((rows, cols + 2 * LANES), f32),
            pltpu.VMEM((pairs, 2 * BASIS, rows, PAIR), f32),
            pltpu.VMEM((2 * N_COL, 2, 3 * reach, PAIR), bf16),
            pltpu.VMEM((3 * rows, PAIR), bf16),
            pltpu.VMEM((pairs, rows, PAIR), f32),
            pltpu.VMEM((32, 8, LANES), f32),
            pltpu.VMEM((groups, 32, LANES), f32),
            pltpu.VMEM((8, LANES), jnp.int32),
            pltpu.VMEM((visits, 8, LANES), jnp.int32),
            pltpu.VMEM(row_ops.shape, bf16),
            pltpu.VMEM(smooth_op.shape, bf16),
            pltpu.VMEM(col_ops.shape, bf16),
            pltpu.VMEM(smooth_cols.shape, bf16),
            pltpu.VMEM(ones_rows.shape, f32),
            pltpu.VMEM(ones_cols.shape[1:], f32),
            dma((9 + chunks,)),
            dma((visits,)),
            dma((visits,)),
            dma((chunks, visits)),
            dma((chunks, visits)),
            dma((chunks, visits)),
            dma((chunks, visits)),
            dma((4,)),
            dma((4,)),
            dma((groups,)),
            dma((groups,)),
        ],
        compiler_params=pltpu.CompilerParams(
            collective_id=0, has_side_effects=True, vmem_limit_bytes=54 * 1024 * 1024
        ),
        name="difference_imaging",
    )(coadd_tiles, science, correlation, offset, *[jnp.asarray(c) for c in consts])
    return pl.pallas_call(
        finish,
        out_shape=(
            jax.ShapeDtypeStruct((rows, cols), f32),
            jax.ShapeDtypeStruct((rows, cols), f32),
            jax.ShapeDtypeStruct((1, BASIS + 1), f32),
        ),
        in_specs=[vmem] * 3,
        out_specs=(anywhere, anywhere, vmem),
        scratch_shapes=[
            pltpu.VMEM((PARTS, rows // PARTS, cols), f32),
            dma((PARTS,)),
            dma,
        ],
        compiler_params=pltpu.CompilerParams(vmem_limit_bytes=8 * 1024 * 1024),
        name="finish",
    )(*[pltpu.with_memory_space_constraint(x, pltpu.VMEM) for x in (difference, filtered, small)])


def solution(mesh):
    in_specs = (P("visit", "grp"), P("visit", "grp"), P("visit"), P("visit"))
    out_specs = (P("visit", "grp"), P("visit", "grp"), P("visit", None))
    return jax.shard_map(shards, mesh=mesh, in_specs=in_specs, out_specs=out_specs, check_vma=False)
```

```python
import functools

import jax
import jax.numpy as jnp
import ml_dtypes
import numpy as np
from jax import lax
from jax.experimental import pallas as pl
from jax.experimental.pallas import tpu as pltpu
from jax.sharding import PartitionSpec as P

KER_HALF = 10
BASIS = 5
FILT_HALF = 6
RIDGE = 0.05
EPSILON = 1e-06

LANES = 128
PAIR = 2 * LANES
SHIFT = KER_HALF + FILT_HALF
MESH = pl.DeviceIdType.MESH

ROW_OF = (0, 1, 2, 3, 1)
COL_OF = (0, 1, 2, 1, 3)
N_COL = 4
N_SUMS = 26
PARTS = 4


def gauss(spread, half):
    points = np.arange(-half, half + 1, dtype=np.float64)
    return np.exp(-points * points / (2.0 * spread * spread))


def operator_taps():
    points = np.arange(-KER_HALF, KER_HALF + 1, dtype=np.float64)
    narrow, middle, wide = (gauss(s, KER_HALF) for s in (1.0, 1.8, 3.2))
    slope = points * middle / 1.8
    rows = (narrow, middle, wide, slope, middle)
    cols = (narrow, middle, wide, middle, slope)
    scales = [np.sqrt(np.sum(r * r) * np.sum(c * c)) for r, c in zip(rows, cols)]
    rows = [r / s for r, s in zip(rows, scales)]
    smooth = gauss(2.0, FILT_HALF)
    smooth = smooth / np.sqrt(np.sum(smooth * smooth))
    col_fields = (narrow, middle, wide, slope)
    return rows, col_fields, smooth


def banded(taps, n_out, n_in, shift):
    half = (len(taps) - 1) // 2
    gap = np.arange(n_in)[None, :] - np.arange(n_out)[:, None] - shift + half
    inside = (gap >= 0) & (gap < len(taps))
    return np.where(inside, taps[np.clip(gap, 0, len(taps) - 1)], 0.0)


def halves(x):
    x = x.astype(np.float32)
    high = x.astype(ml_dtypes.bfloat16)
    low = (x - high.astype(np.float32)).astype(ml_dtypes.bfloat16)
    return high, low


def row_stack(mats, depth):
    out = []
    for mat in mats:
        full = np.zeros((mat.shape[0], depth))
        full[:, : mat.shape[1]] = mat
        high, low = halves(full)
        out.append(np.concatenate([high, high, low], 1))
    return np.stack(out)


def lower_start(rows):
    return rows // 2 - 8


def halved_rows(mats, rows, reach):
    upper = row_stack([m[: rows // 2, :reach] for m in mats], reach)
    low = lower_start(rows)
    lower = row_stack([m[rows // 2 :, low : low + reach] for m in mats], reach)
    return np.stack([upper, lower])


def constants(rows, cols, groups, reach):
    row_taps, col_taps, smooth = operator_taps()
    smooth_rows = banded(smooth, rows, rows, 0)
    span = rows + 2 * KER_HALF
    plain = [banded(r, rows, span, KER_HALF) for r in row_taps]
    row_ops = halved_rows(plain + [smooth_rows @ m for m in plain], rows, reach)
    smooth_op = row_stack([smooth_rows], rows)[0]

    def column_mats(keep_left, keep_right):
        wide = LANES + 2 * FILT_HALF
        keep = np.ones(wide)
        if not keep_left:
            keep[:FILT_HALF] = 0.0
        if not keep_right:
            keep[wide - FILT_HALF :] = 0.0
        gather = banded(smooth, LANES, wide, FILT_HALF) * keep[None, :]
        mats = [banded(c, LANES, PAIR, SHIFT) for c in col_taps]
        mats += [gather @ banded(c, wide, PAIR, SHIFT - FILT_HALF) for c in col_taps]
        return np.concatenate([m.T for m in mats], 1)

    def packed(mat):
        return np.stack(halves(mat))

    inner = packed(column_mats(True, True))
    left = packed(column_mats(False, True))
    right = packed(column_mats(True, False))
    col_ops = np.stack([inner, left, right])
    smooth_cols = packed(banded(smooth, LANES, PAIR, SHIFT).T)

    ones_rows = np.broadcast_to(smooth_rows.sum(1)[:, None], (rows, LANES))
    ones_cols = []
    for group in range(groups):
        columns = np.arange(cols)[:, None] + np.arange(-FILT_HALF, FILT_HALF + 1)[None, :]
        inside = (columns + group * cols >= 0) & (columns + group * cols < groups * cols)
        ones_cols.append(np.broadcast_to((inside * smooth).sum(1)[None], (8, cols)))
    return (
        row_ops,
        smooth_op,
        col_ops,
        smooth_cols,
        ones_rows.astype(np.float32),
        np.stack(ones_cols).astype(np.float32),
    )


def split(x):
    high = x.astype(jnp.bfloat16)
    low = (x - high.astype(jnp.float32)).astype(jnp.bfloat16)
    return high, low


def dot(a, b):
    return jnp.dot(a, b, preferred_element_type=jnp.float32)


def kernel(
    visits,
    groups,
    tiles_ref,
    science_ref,
    correlation_ref,
    offset_ref,
    row_ops_ref,
    smooth_op_ref,
    col_ops_ref,
    smooth_cols_ref,
    ones_rows_ref,
    ones_cols_ref,
    difference_ref,
    filtered_ref,
    small_ref,
    strip,
    outgoing,
    window,
    science,
    fields,
    stage,
    smooth_stage,
    smoothed,
    sums,
    totals,
    place,
    places,
    row_ops,
    smooth_op,
    col_ops,
    smooth_cols,
    ones_rows,
    ones_cols,
    load_sems,
    place_send,
    place_recv,
    first_send,
    first_recv,
    second_send,
    second_recv,
    halo_send,
    halo_recv,
    total_send,
    total_recv,
):
    rows, cols = tiles_ref.shape
    blocks = cols // LANES
    pairs = blocks // 2
    chunks = blocks // visits
    half = visits // 2
    depth = window.shape[1]
    sent = outgoing.shape[2]
    reach = sent - lower_start(rows)
    me = lax.axis_index("visit")
    group = lax.axis_index("grp")
    has_left = group > 0
    has_right = group < groups - 1

    def block_of(chunk, owner):
        if chunk == 0:
            return owner + (owner // half) * (blocks - visits)
        return half + owner

    def lane(block):
        return pl.ds(pl.multiple_of(block * LANES, LANES), LANES)

    def other_visit(step):
        return lax.rem(me + step, visits)

    at_left = jnp.where(group == 0, 1, 0)
    at_right = jnp.where(group == groups - 1, 2, 0)
    loads = [
        (science_ref, science.at[:, pl.ds(LANES, cols)]),
        (smooth_op_ref, smooth_op),
        (smooth_cols_ref, smooth_cols),
        (row_ops_ref, row_ops),
        (col_ops_ref.at[0], col_ops.at[0]),
        (col_ops_ref.at[at_left], col_ops.at[1]),
        (col_ops_ref.at[at_right], col_ops.at[2]),
        (ones_rows_ref, ones_rows),
        (ones_cols_ref.at[group], ones_cols),
    ]
    for chunk in range(chunks):
        loads.append(
            (
                tiles_ref.at[:, lane(block_of(chunk, me))],
                strip[chunk].at[pl.ds(pl.multiple_of(me * rows, rows), rows), :],
            )
        )
    loads = [pltpu.make_async_copy(a, b, load_sems.at[i]) for i, (a, b) in enumerate(loads)]

    barrier = pltpu.get_barrier_semaphore()
    for step in range(1, visits):
        pl.semaphore_signal(
            barrier, inc=1, device_id=(other_visit(step), group), device_id_type=MESH
        )
    for step in range(1, groups):
        pl.semaphore_signal(
            barrier,
            inc=1,
            device_id=(me, lax.rem(group + step, groups)),
            device_id_type=MESH,
        )
    strip_rows = visits * rows
    first_row = correlation_ref[0] * rows + offset_ref[0] - KER_HALF
    first_row = lax.rem(first_row + strip_rows, strip_rows)
    place[...] = jnp.full(place.shape, first_row, jnp.int32)
    places[me] = jnp.full(place.shape, first_row, jnp.int32)
    window[:, sent:, :] = jnp.zeros((blocks + 2, depth - sent, LANES), jnp.float32)
    pl.semaphore_wait(barrier, visits - 1 + groups - 1)

    def place_copy(step, source=None):
        return pltpu.make_async_remote_copy(
            src_ref=place,
            dst_ref=places.at[me if source is None else source],
            send_sem=place_send.at[step],
            recv_sem=place_recv.at[me if source is None else source],
            device_id=(other_visit(step), group),
            device_id_type=MESH,
        )

    def first_copy(chunk, step, source=None):
        target = other_visit(step)
        source = me if source is None else source
        return pltpu.make_async_remote_copy(
            src_ref=tiles_ref.at[:, lane(block_of(chunk, target))],
            dst_ref=strip[chunk].at[pl.ds(pl.multiple_of(source * rows, rows), rows), :],
            send_sem=first_send.at[chunk, step],
            recv_sem=first_recv.at[chunk, source],
            device_id=(target, group),
            device_id_type=MESH,
        )

    def second_copy(chunk, step, source=None):
        target = other_visit(step)
        source = me if source is None else source
        return pltpu.make_async_remote_copy(
            src_ref=outgoing.at[chunk, target],
            dst_ref=window.at[block_of(chunk, source) + 1, pl.ds(0, sent), :],
            send_sem=second_send.at[chunk, step],
            recv_sem=second_recv.at[chunk, source],
            device_id=(target, group),
            device_id_type=MESH,
        )

    def halo_copy(index, source, target, neighbour):
        return pltpu.make_async_remote_copy(
            src_ref=source,
            dst_ref=target,
            send_sem=halo_send.at[index],
            recv_sem=halo_recv.at[index],
            device_id=(me, neighbour),
            device_id_type=MESH,
        )

    left = lax.rem(group + groups - 1, groups)
    right = lax.rem(group + 1, groups)
    last = blocks * LANES
    science_right = halo_copy(
        0, science_ref.at[:, pl.ds(last - LANES, LANES)], science.at[:, pl.ds(0, LANES)], right
    )
    science_left = halo_copy(
        1, science_ref.at[:, pl.ds(0, LANES)], science.at[:, pl.ds(last + LANES, LANES)], left
    )
    window_right = halo_copy(
        2, window.at[blocks, pl.ds(0, sent), :], window.at[0, pl.ds(0, sent), :], right
    )
    window_left = halo_copy(
        3, window.at[1, pl.ds(0, sent), :], window.at[blocks + 1, pl.ds(0, sent), :], left
    )

    for step in range(1, visits):
        place_copy(step).start()
    for chunk in range(chunks):
        for step in range(1, visits):
            first_copy(chunk, step).start()

    @pl.when(has_right)
    def _():
        science_right.start()

    @pl.when(has_left)
    def _():
        science_left.start()

    for load in loads:
        load.start()

    @pl.when(jnp.logical_not(has_left))
    def _():
        science[:, 0:LANES] = jnp.zeros((rows, LANES), jnp.float32)
        window[0, 0:sent, :] = jnp.zeros((sent, LANES), jnp.float32)

    @pl.when(jnp.logical_not(has_right))
    def _():
        science[:, last + LANES :] = jnp.zeros((rows, LANES), jnp.float32)
        window[blocks + 1, 0:sent, :] = jnp.zeros((sent, LANES), jnp.float32)

    sums[...] = jnp.zeros(sums.shape, jnp.float32)
    for load in loads:
        load.wait()

    @pl.when(has_left)
    def _():
        science_right.wait_recv()

    @pl.when(has_right)
    def _():
        science_left.wait_recv()

    def science_pair(pair, carry):
        four = science[:, pl.ds(pl.multiple_of(pair * PAIR, PAIR), 2 * PAIR)]
        four = pltpu.roll(four, 2 * PAIR - (LANES - SHIFT), 1)
        high, low = split(four)
        for j in range(2):
            at = slice(j * LANES, j * LANES + PAIR)
            field = (
                dot(high[:, at], smooth_cols[0])
                + dot(low[:, at], smooth_cols[0])
                + dot(high[:, at], smooth_cols[1])
            )
            h, l = split(field)
            out = slice(j * LANES, (j + 1) * LANES)
            smooth_stage[0:rows, out] = h
            smooth_stage[rows : 2 * rows, out] = l
            smooth_stage[2 * rows : 3 * rows, out] = h
        smoothed[pair] = dot(smooth_op[...], smooth_stage[...])
        return carry

    lax.fori_loop(0, pairs, science_pair, 0)

    for step in range(1, visits):
        place_copy(step, other_visit(step)).wait_recv()
    for chunk in range(chunks):
        for step in range(1, visits):
            first_copy(chunk, step, other_visit(step)).wait_recv()
        end = visits * rows
        extra = strip[chunk].shape[0] - end
        strip[chunk][end:, :] = strip[chunk][0:extra, :]

        def cut(step, carry):
            target = lax.rem(me + step, visits)
            start = places[target][0, 0]
            outgoing[chunk, target] = strip[chunk][pl.ds(start, sent), :]
            return carry

        for step in range(1, visits):
            cut(step, 0)
            second_copy(chunk, step).start()
        window[block_of(chunk, me) + 1, 0:sent, :] = strip[chunk][
            pl.ds(places[me][0, 0], sent), :
        ]

    def wait_block(chunk, owner):
        @pl.when(owner != me)
        def _():
            second_copy(chunk, 1, owner).wait_recv()

    in_left = me < half
    staged = chunks == 2 and visits == 8

    def blocks_of(pair):
        return 2 * pair + 1, (2 * pair + 2) % blocks

    def pair_of(block):
        return (block - 1) // 2 % pairs, (block - 1) % 2


    def exposure_pair(index, carry):
        @pl.when(index == 0)
        def _():
            wait_block(0, 0)
            wait_block(0, visits - 1)

            @pl.when(has_right)
            def _():
                window_right.start()

            @pl.when(has_left)
            def _():
                window_left.start()

            for owner in range(1, visits - 1):
                wait_block(0, owner)
            if not staged:
                for chunk in range(1, chunks):
                    for owner in range(visits):
                        wait_block(chunk, owner)

            @pl.when(has_left)
            def _():
                window_right.wait_recv()

            @pl.when(has_right)
            def _():
                window_left.wait_recv()

        pair = jnp.where(index == 0, pairs - 1, jnp.where(index == 1, 0, index - 2))
        pair = jnp.where(index == 2, pairs - 2, pair)
        pair = jnp.where((index > 2) & (index <= half), index - 2, pair)
        pair = jnp.where(index > half, pairs + half - 2 - index, pair)
        pair = jnp.where(in_left | (pair == pairs - 1), pair, pairs - 2 - pair)

        if staged:
            for k, first in enumerate((0, 2, visits - 2, visits - 4)):

                @pl.when(index == 3 + k)
                def _(first=first):
                    for owner in (first, first + 1):
                        wait_block(1, jnp.where(in_left, owner, visits - 1 - owner))

        for j, block in enumerate(blocks_of(pair)):
            three = jnp.concatenate([window[block + k] for k in range(3)], 1)
            three = pltpu.roll(three, 2 * LANES + SHIFT, 1)[:, :PAIR]
            high, low = split(three)
            which = jnp.where(block == 0, 1, jnp.where(block == blocks - 1, 2, 0))
            field = (
                dot(high, col_ops[which, 0])
                + dot(low, col_ops[which, 0])
                + dot(high, col_ops[which, 1])
            )
            out = slice(j * LANES, (j + 1) * LANES)
            for f in range(2 * N_COL):
                for part in range(2):
                    first = part * lower_start(rows)
                    h, l = split(field[first : first + reach, f * LANES : (f + 1) * LANES])
                    stage[f, part, 0:reach, out] = h
                    stage[f, part, reach : 2 * reach, out] = l
                    stage[f, part, 2 * reach : 3 * reach, out] = h
        for part in range(2):
            into = slice(part * (rows // 2), (part + 1) * (rows // 2))
            for f in range(2 * N_COL):
                made = [b + BASIS * (f // N_COL) for b in range(BASIS) if COL_OF[b] == f % N_COL]
                ops = [row_ops[part, at] for at in made]
                ops = ops[0] if len(ops) == 1 else jnp.concatenate(ops, 0)
                image = dot(ops, stage[f, part])
                for k, at in enumerate(made):
                    fields[pair, at, into, :] = image[k * (rows // 2) : (k + 1) * (rows // 2)]

        def gather(slab, acc):
            at = pl.ds(pl.multiple_of(slab * 8, 8), 8)
            acc = list(acc)
            for j, block in enumerate(blocks_of(pair)):
                cut_at = slice(j * LANES, (j + 1) * LANES)
                m = [fields[pair, b, at, cut_at] for b in range(BASIS)]
                s = science[at, lane(block + 1)]
                terms = [m[b] * m[c] for b in range(BASIS) for c in range(b, BASIS)]
                terms += m + [m[b] * s for b in range(BASIS)] + [s]
                acc = [a + t for a, t in zip(acc, terms)]
            return tuple(acc)

        acc = tuple(sums[k] for k in range(N_SUMS))
        acc = lax.fori_loop(0, rows // 8, gather, acc, unroll=4)
        for k in range(N_SUMS):
            sums[k] = acc[k]
        return carry

    lax.fori_loop(0, pairs, exposure_pair, 0)

    totals[group] = jnp.sum(sums[...], axis=1)

    def total_copy(step, source=None):
        source = group if source is None else source
        return pltpu.make_async_remote_copy(
            src_ref=totals.at[source],
            dst_ref=totals.at[source],
            send_sem=total_send.at[step],
            recv_sem=total_recv.at[source],
            device_id=(me, lax.rem(group + step, groups)),
            device_id_type=MESH,
        )

    for step in range(1, groups):
        total_copy(step).start()
    for step in range(1, groups):
        total_copy(step, lax.rem(group + step, groups)).wait_recv()
    total = totals[0]
    for g in range(1, groups):
        total = total + totals[g]
    counted = float(rows * cols * groups)
    total = jnp.sum(total, axis=1, keepdims=True) / counted
    entry = [jnp.broadcast_to(total[k : k + 1, :], (8, LANES)) for k in range(N_SUMS)]

    size = BASIS + 1
    normal = {}
    at = 0
    for b in range(BASIS):
        for c in range(b, BASIS):
            normal[b, c] = entry[at] + RIDGE if b == c else entry[at]
            at += 1
    for b in range(BASIS):
        normal[b, BASIS] = entry[at + b]
    normal[BASIS, BASIS] = jnp.full((8, LANES), 1.0 + RIDGE, jnp.float32)
    rhs = [entry[at + BASIS + b] for b in range(size)]
    inverse = []
    for k in range(size):
        inverse.append(1.0 / normal[k, k])
        for i in range(k + 1, size):
            factor = normal[k, i] * inverse[k]
            for j in range(i, size):
                normal[i, j] = normal[i, j] - factor * normal[k, j]
            rhs[i] = rhs[i] - factor * rhs[k]
    coef = [None] * size
    for k in reversed(range(size)):
        value = rhs[k]
        for j in range(k + 1, size):
            value = value - normal[k, j] * coef[j]
        coef[k] = value * inverse[k]

    def combine(slab, power):
        at = pl.ds(pl.multiple_of(slab * 8, 8), 8)
        edge = coef[BASIS] * ones_rows[at, :]
        for block in range(blocks):
            pair, j = pair_of(block)
            cut_at = slice(j * LANES, (j + 1) * LANES)
            even_at = slice(block % 2 * LANES, (block % 2 + 1) * LANES)
            first = block * LANES
            s = science[at, first + LANES : first + 2 * LANES]
            f = smoothed[block // 2, at, even_at] - edge * ones_cols[:, first : first + LANES]
            m = coef[0] * fields[pair, 0, at, cut_at]
            g = coef[0] * fields[pair, BASIS, at, cut_at]
            for b in range(1, BASIS):
                m = m + coef[b] * fields[pair, b, at, cut_at]
                g = g + coef[b] * fields[pair, BASIS + b, at, cut_at]
            partial = s - m
            whole = partial - coef[BASIS]
            difference_ref[at, first : first + LANES] = whole
            filtered_ref[at, first : first + LANES] = f - g
            power = power + whole * whole
        return power

    power = lax.fori_loop(0, rows // 8, combine, jnp.zeros((8, LANES), jnp.float32))
    power = jnp.sum(jnp.sum(power, axis=1, keepdims=True), axis=0, keepdims=True)
    scale = 1.0 / jnp.sqrt(power / float(rows * cols) + EPSILON)
    column = lax.broadcasted_iota(jnp.int32, (8, LANES), 1)
    row = lax.broadcasted_iota(jnp.int32, (8, LANES), 0)
    small = jnp.broadcast_to(scale, (8, LANES))
    for k in range(size):
        small = jnp.where((row == 0) & (column == k), coef[k], small)
    small_ref[...] = small

    for step in range(1, visits):
        place_copy(step).wait_send()
        for chunk in range(chunks):
            first_copy(chunk, step).wait_send()
            second_copy(chunk, step).wait_send()
    for step in range(1, groups):
        total_copy(step).wait_send()

    @pl.when(has_right)
    def _():
        science_right.wait_send()
        window_right.wait_send()

    @pl.when(has_left)
    def _():
        science_left.wait_send()
        window_left.wait_send()


def finish(difference, filtered, small, difference_ref, significance_ref, coef_ref, scaled, sems, sem):
    out = pltpu.make_async_copy(difference, difference_ref, sem)
    out.start()
    scale = small[1:2, 0:1]
    size = difference.shape[0] // PARTS
    copies = []
    for part in range(PARTS):
        at = pl.ds(part * size, size)
        scaled[part] = filtered[at, :] * scale
        copies.append(
            pltpu.make_async_copy(scaled.at[part], significance_ref.at[at, :], sems.at[part])
        )
        copies[-1].start()
    coef_ref[...] = small[0:1, 0 : BASIS + 1]
    out.wait()
    for copy in copies:
        copy.wait()


def shards(coadd_tiles, science, correlation, offset):
    visits = lax.axis_size("visit")
    groups = lax.axis_size("grp")
    rows, cols = coadd_tiles.shape
    blocks = cols // LANES
    pairs = blocks // 2
    chunks = blocks // visits
    span = rows + 2 * KER_HALF
    sent = -(-span // 8) * 8
    depth = -(-span // 16) * 16
    reach = sent - lower_start(rows)
    consts = constants(rows, cols, groups, reach)
    row_ops, smooth_op, col_ops, smooth_cols, ones_rows, ones_cols = consts
    f32, bf16 = jnp.float32, jnp.bfloat16
    anywhere = pl.BlockSpec(memory_space=pl.ANY)
    scalar = pl.BlockSpec(memory_space=pltpu.SMEM)
    vmem = pl.BlockSpec(memory_space=pltpu.VMEM)
    dma = pltpu.SemaphoreType.DMA
    difference, filtered, small = pl.pallas_call(
        functools.partial(kernel, visits, groups),
        out_shape=(
            pltpu.VMEM((rows, cols), f32),
            pltpu.VMEM((rows, cols), f32),
            pltpu.VMEM((8, LANES), f32),
        ),
        in_specs=[anywhere, anywhere, scalar, scalar] + [anywhere] * 6,
        out_specs=(vmem, vmem, vmem),
        scratch_shapes=[
            (pltpu.VMEM((visits * rows + sent, LANES), f32),) * chunks,
            pltpu.VMEM((chunks, visits, sent, LANES), f32),
            pltpu.VMEM((blocks + 2, depth, LANES), f32),
            pltpu.VMEM((rows, cols + 2 * LANES), f32),
            pltpu.VMEM((pairs, 2 * BASIS, rows, PAIR), f32),
            pltpu.VMEM((2 * N_COL, 2, 3 * reach, PAIR), bf16),
            pltpu.VMEM((3 * rows, PAIR), bf16),
            pltpu.VMEM((pairs, rows, PAIR), f32),
            pltpu.VMEM((32, 8, LANES), f32),
            pltpu.VMEM((groups, 32, LANES), f32),
            pltpu.VMEM((8, LANES), jnp.int32),
            pltpu.VMEM((visits, 8, LANES), jnp.int32),
            pltpu.VMEM(row_ops.shape, bf16),
            pltpu.VMEM(smooth_op.shape, bf16),
            pltpu.VMEM(col_ops.shape, bf16),
            pltpu.VMEM(smooth_cols.shape, bf16),
            pltpu.VMEM(ones_rows.shape, f32),
            pltpu.VMEM(ones_cols.shape[1:], f32),
            dma((9 + chunks,)),
            dma((visits,)),
            dma((visits,)),
            dma((chunks, visits)),
            dma((chunks, visits)),
            dma((chunks, visits)),
            dma((chunks, visits)),
            dma((4,)),
            dma((4,)),
            dma((groups,)),
            dma((groups,)),
        ],
        compiler_params=pltpu.CompilerParams(
            collective_id=0, has_side_effects=True, vmem_limit_bytes=54 * 1024 * 1024
        ),
        name="difference_imaging",
    )(coadd_tiles, science, correlation, offset, *[jnp.asarray(c) for c in consts])
    return pl.pallas_call(
        finish,
        out_shape=(
            jax.ShapeDtypeStruct((rows, cols), f32),
            jax.ShapeDtypeStruct((rows, cols), f32),
            jax.ShapeDtypeStruct((1, BASIS + 1), f32),
        ),
        in_specs=[vmem] * 3,
        out_specs=(anywhere, anywhere, vmem),
        scratch_shapes=[
            pltpu.VMEM((PARTS, rows // PARTS, cols), f32),
            dma((PARTS,)),
            dma,
        ],
        compiler_params=pltpu.CompilerParams(vmem_limit_bytes=8 * 1024 * 1024),
        name="finish",
    )(*[pltpu.with_memory_space_constraint(x, pltpu.VMEM) for x in (difference, filtered, small)])


def solution(mesh):
    in_specs = (P("visit", "grp"), P("visit", "grp"), P("visit"), P("visit"))
    out_specs = (P("visit", "grp"), P("visit", "grp"), P("visit", None))
    return jax.shard_map(shards, mesh=mesh, in_specs=in_specs, out_specs=out_specs, check_vma=False)
```

```python
import functools

import jax
import jax.numpy as jnp
import ml_dtypes
import numpy as np
from jax import lax
from jax.experimental import pallas as pl
from jax.experimental.pallas import tpu as pltpu
from jax.sharding import PartitionSpec as P

KER_HALF = 10
BASIS = 5
FILT_HALF = 6
RIDGE = 0.05
EPSILON = 1e-06

LANES = 128
PAIR = 2 * LANES
SHIFT = KER_HALF + FILT_HALF
MESH = pl.DeviceIdType.MESH

ROW_OF = (0, 1, 2, 3, 1)
COL_OF = (0, 1, 2, 1, 3)
N_COL = 4
N_SUMS = 26
PARTS = 4


def gauss(spread, half):
    points = np.arange(-half, half + 1, dtype=np.float64)
    return np.exp(-points * points / (2.0 * spread * spread))


def operator_taps():
    points = np.arange(-KER_HALF, KER_HALF + 1, dtype=np.float64)
    narrow, middle, wide = (gauss(s, KER_HALF) for s in (1.0, 1.8, 3.2))
    slope = points * middle / 1.8
    rows = (narrow, middle, wide, slope, middle)
    cols = (narrow, middle, wide, middle, slope)
    scales = [np.sqrt(np.sum(r * r) * np.sum(c * c)) for r, c in zip(rows, cols)]
    rows = [r / s for r, s in zip(rows, scales)]
    smooth = gauss(2.0, FILT_HALF)
    smooth = smooth / np.sqrt(np.sum(smooth * smooth))
    col_fields = (narrow, middle, wide, slope)
    return rows, col_fields, smooth


def banded(taps, n_out, n_in, shift):
    half = (len(taps) - 1) // 2
    gap = np.arange(n_in)[None, :] - np.arange(n_out)[:, None] - shift + half
    inside = (gap >= 0) & (gap < len(taps))
    return np.where(inside, taps[np.clip(gap, 0, len(taps) - 1)], 0.0)


def halves(x):
    x = x.astype(np.float32)
    high = x.astype(ml_dtypes.bfloat16)
    low = (x - high.astype(np.float32)).astype(ml_dtypes.bfloat16)
    return high, low


def row_stack(mats, depth):
    out = []
    for mat in mats:
        full = np.zeros((mat.shape[0], depth))
        full[:, : mat.shape[1]] = mat
        high, low = halves(full)
        out.append(np.concatenate([high, high, low], 1))
    return np.stack(out)


def lower_start(rows):
    return rows // 2 - 8


def halved_rows(mats, rows, reach):
    upper = row_stack([m[: rows // 2, :reach] for m in mats], reach)
    low = lower_start(rows)
    lower = row_stack([m[rows // 2 :, low : low + reach] for m in mats], reach)
    return np.stack([upper, lower])


def constants(rows, cols, groups, reach):
    row_taps, col_taps, smooth = operator_taps()
    smooth_rows = banded(smooth, rows, rows, 0)
    span = rows + 2 * KER_HALF
    plain = [banded(r, rows, span, KER_HALF) for r in row_taps]
    row_ops = halved_rows(plain + [smooth_rows @ m for m in plain], rows, reach)
    smooth_op = row_stack([smooth_rows], rows)[0]

    def column_mats(keep_left, keep_right):
        wide = LANES + 2 * FILT_HALF
        keep = np.ones(wide)
        if not keep_left:
            keep[:FILT_HALF] = 0.0
        if not keep_right:
            keep[wide - FILT_HALF :] = 0.0
        gather = banded(smooth, LANES, wide, FILT_HALF) * keep[None, :]
        mats = [banded(c, LANES, PAIR, SHIFT) for c in col_taps]
        mats += [gather @ banded(c, wide, PAIR, SHIFT - FILT_HALF) for c in col_taps]
        return np.concatenate([m.T for m in mats], 1)

    def packed(mat):
        return np.stack(halves(mat))

    inner = packed(column_mats(True, True))
    left = packed(column_mats(False, True))
    right = packed(column_mats(True, False))
    col_ops = np.stack([inner, left, right])
    smooth_cols = packed(banded(smooth, LANES, PAIR, SHIFT).T)

    ones_rows = np.broadcast_to(smooth_rows.sum(1)[:, None], (rows, LANES))
    ones_cols = []
    for group in range(groups):
        columns = np.arange(cols)[:, None] + np.arange(-FILT_HALF, FILT_HALF + 1)[None, :]
        inside = (columns + group * cols >= 0) & (columns + group * cols < groups * cols)
        ones_cols.append(np.broadcast_to((inside * smooth).sum(1)[None], (8, cols)))
    return (
        row_ops,
        smooth_op,
        col_ops,
        smooth_cols,
        ones_rows.astype(np.float32),
        np.stack(ones_cols).astype(np.float32),
    )


def split(x):
    high = x.astype(jnp.bfloat16)
    low = (x - high.astype(jnp.float32)).astype(jnp.bfloat16)
    return high, low


def dot(a, b):
    return jnp.dot(a, b, preferred_element_type=jnp.float32)


def kernel(
    visits,
    groups,
    tiles_ref,
    science_ref,
    correlation_ref,
    offset_ref,
    row_ops_ref,
    smooth_op_ref,
    col_ops_ref,
    smooth_cols_ref,
    ones_rows_ref,
    ones_cols_ref,
    difference_ref,
    filtered_ref,
    small_ref,
    strip,
    outgoing,
    window,
    science,
    fields,
    stage,
    smooth_stage,
    smoothed,
    sums,
    totals,
    place,
    places,
    row_ops,
    smooth_op,
    col_ops,
    smooth_cols,
    ones_rows,
    ones_cols,
    load_sems,
    place_send,
    place_recv,
    first_send,
    first_recv,
    second_send,
    second_recv,
    halo_send,
    halo_recv,
    total_send,
    total_recv,
):
    rows, cols = tiles_ref.shape
    blocks = cols // LANES
    pairs = blocks // 2
    chunks = blocks // visits
    half = visits // 2
    depth = window.shape[1]
    sent = outgoing.shape[2]
    reach = -(-sent // 8) * 8 - lower_start(rows)
    me = lax.axis_index("visit")
    group = lax.axis_index("grp")
    has_left = group > 0
    has_right = group < groups - 1

    def block_of(chunk, owner):
        if chunk == 0:
            return owner + (owner // half) * (blocks - visits)
        return half + owner

    def lane(block):
        return pl.ds(pl.multiple_of(block * LANES, LANES), LANES)

    def other_visit(step):
        return lax.rem(me + step, visits)

    at_left = jnp.where(group == 0, 1, 0)
    at_right = jnp.where(group == groups - 1, 2, 0)
    loads = [
        (science_ref, science.at[:, pl.ds(LANES, cols)]),
        (smooth_op_ref, smooth_op),
        (smooth_cols_ref, smooth_cols),
        (row_ops_ref, row_ops),
        (col_ops_ref.at[0], col_ops.at[0]),
        (col_ops_ref.at[at_left], col_ops.at[1]),
        (col_ops_ref.at[at_right], col_ops.at[2]),
        (ones_rows_ref, ones_rows),
        (ones_cols_ref.at[group], ones_cols),
    ]
    for chunk in range(chunks):
        loads.append(
            (
                tiles_ref.at[:, lane(block_of(chunk, me))],
                strip[chunk].at[pl.ds(pl.multiple_of(me * rows, rows), rows), :],
            )
        )
    loads = [pltpu.make_async_copy(a, b, load_sems.at[i]) for i, (a, b) in enumerate(loads)]

    barrier = pltpu.get_barrier_semaphore()
    for step in range(1, visits):
        pl.semaphore_signal(
            barrier, inc=1, device_id=(other_visit(step), group), device_id_type=MESH
        )
    for step in range(1, groups):
        pl.semaphore_signal(
            barrier,
            inc=1,
            device_id=(me, lax.rem(group + step, groups)),
            device_id_type=MESH,
        )
    strip_rows = visits * rows
    first_row = correlation_ref[0] * rows + offset_ref[0] - KER_HALF
    first_row = lax.rem(first_row + strip_rows, strip_rows)
    place[...] = jnp.full(place.shape, first_row, jnp.int32)
    places[me] = jnp.full(place.shape, first_row, jnp.int32)
    window[:, sent:, :] = jnp.zeros((blocks + 2, depth - sent, LANES), jnp.float32)
    pl.semaphore_wait(barrier, visits - 1 + groups - 1)

    def place_copy(step, source=None):
        return pltpu.make_async_remote_copy(
            src_ref=place,
            dst_ref=places.at[me if source is None else source],
            send_sem=place_send.at[step],
            recv_sem=place_recv.at[me if source is None else source],
            device_id=(other_visit(step), group),
            device_id_type=MESH,
        )

    def first_copy(chunk, step, source=None):
        target = other_visit(step)
        source = me if source is None else source
        return pltpu.make_async_remote_copy(
            src_ref=tiles_ref.at[:, lane(block_of(chunk, target))],
            dst_ref=strip[chunk].at[pl.ds(pl.multiple_of(source * rows, rows), rows), :],
            send_sem=first_send.at[chunk, step],
            recv_sem=first_recv.at[chunk, source],
            device_id=(target, group),
            device_id_type=MESH,
        )

    def second_copy(chunk, step, source=None):
        target = other_visit(step)
        source = me if source is None else source
        return pltpu.make_async_remote_copy(
            src_ref=outgoing.at[chunk, target],
            dst_ref=window.at[block_of(chunk, source) + 1, pl.ds(0, sent), :],
            send_sem=second_send.at[chunk, step],
            recv_sem=second_recv.at[chunk, source],
            device_id=(target, group),
            device_id_type=MESH,
        )

    def halo_copy(index, source, target, neighbour):
        return pltpu.make_async_remote_copy(
            src_ref=source,
            dst_ref=target,
            send_sem=halo_send.at[index],
            recv_sem=halo_recv.at[index],
            device_id=(me, neighbour),
            device_id_type=MESH,
        )

    left = lax.rem(group + groups - 1, groups)
    right = lax.rem(group + 1, groups)
    last = blocks * LANES
    science_right = halo_copy(
        0, science_ref.at[:, pl.ds(last - LANES, LANES)], science.at[:, pl.ds(0, LANES)], right
    )
    science_left = halo_copy(
        1, science_ref.at[:, pl.ds(0, LANES)], science.at[:, pl.ds(last + LANES, LANES)], left
    )
    window_right = halo_copy(
        2, window.at[blocks, pl.ds(0, sent), :], window.at[0, pl.ds(0, sent), :], right
    )
    window_left = halo_copy(
        3, window.at[1, pl.ds(0, sent), :], window.at[blocks + 1, pl.ds(0, sent), :], left
    )

    for step in range(1, visits):
        place_copy(step).start()
    for chunk in range(chunks):
        for step in range(1, visits):
            first_copy(chunk, step).start()

    @pl.when(has_right)
    def _():
        science_right.start()

    @pl.when(has_left)
    def _():
        science_left.start()

    for load in loads:
        load.start()

    @pl.when(jnp.logical_not(has_left))
    def _():
        science[:, 0:LANES] = jnp.zeros((rows, LANES), jnp.float32)
        window[0, 0:sent, :] = jnp.zeros((sent, LANES), jnp.float32)

    @pl.when(jnp.logical_not(has_right))
    def _():
        science[:, last + LANES :] = jnp.zeros((rows, LANES), jnp.float32)
        window[blocks + 1, 0:sent, :] = jnp.zeros((sent, LANES), jnp.float32)

    sums[...] = jnp.zeros(sums.shape, jnp.float32)
    for load in loads:
        load.wait()

    @pl.when(has_left)
    def _():
        science_right.wait_recv()

    @pl.when(has_right)
    def _():
        science_left.wait_recv()

    def science_pair(pair, carry):
        four = science[:, pl.ds(pl.multiple_of(pair * PAIR, PAIR), 2 * PAIR)]
        four = pltpu.roll(four, 2 * PAIR - (LANES - SHIFT), 1)
        high, low = split(four)
        for j in range(2):
            at = slice(j * LANES, j * LANES + PAIR)
            field = (
                dot(high[:, at], smooth_cols[0])
                + dot(low[:, at], smooth_cols[0])
                + dot(high[:, at], smooth_cols[1])
            )
            h, l = split(field)
            out = slice(j * LANES, (j + 1) * LANES)
            smooth_stage[0:rows, out] = h
            smooth_stage[rows : 2 * rows, out] = l
            smooth_stage[2 * rows : 3 * rows, out] = h
        smoothed[pair] = dot(smooth_op[...], smooth_stage[...])
        return carry

    lax.fori_loop(0, pairs, science_pair, 0)

    for step in range(1, visits):
        place_copy(step, other_visit(step)).wait_recv()
    for chunk in range(chunks):
        for step in range(1, visits):
            first_copy(chunk, step, other_visit(step)).wait_recv()
        end = visits * rows
        extra = strip[chunk].shape[0] - end
        strip[chunk][end:, :] = strip[chunk][0:extra, :]

        def cut(step, carry):
            target = lax.rem(me + step, visits)
            start = places[target][0, 0]
            outgoing[chunk, target] = strip[chunk][pl.ds(start, sent), :]
            return carry

        for step in range(1, visits):
            cut(step, 0)
            second_copy(chunk, step).start()
        window[block_of(chunk, me) + 1, 0:sent, :] = strip[chunk][
            pl.ds(places[me][0, 0], sent), :
        ]

    def wait_block(chunk, owner):
        @pl.when(owner != me)
        def _():
            second_copy(chunk, 1, owner).wait_recv()

    in_left = me < half
    staged = chunks == 2 and visits == 8

    def blocks_of(pair):
        return 2 * pair + 1, (2 * pair + 2) % blocks

    def pair_of(block):
        return (block - 1) // 2 % pairs, (block - 1) % 2


    def exposure_pair(index, carry):
        @pl.when(index == 0)
        def _():
            wait_block(0, 0)
            wait_block(0, visits - 1)

            @pl.when(has_right)
            def _():
                window_right.start()

            @pl.when(has_left)
            def _():
                window_left.start()

            for owner in range(1, visits - 1):
                wait_block(0, owner)
            if not staged:
                for chunk in range(1, chunks):
                    for owner in range(visits):
                        wait_block(chunk, owner)

            @pl.when(has_left)
            def _():
                window_right.wait_recv()

            @pl.when(has_right)
            def _():
                window_left.wait_recv()

        pair = jnp.where(index == 0, pairs - 1, jnp.where(index == 1, 0, index - 2))
        pair = jnp.where(index == 2, pairs - 2, pair)
        pair = jnp.where((index > 2) & (index <= half), index - 2, pair)
        pair = jnp.where(index > half, pairs + half - 2 - index, pair)
        pair = jnp.where(in_left | (pair == pairs - 1), pair, pairs - 2 - pair)

        if staged:
            for k, first in enumerate((0, 2, visits - 2, visits - 4)):

                @pl.when(index == 3 + k)
                def _(first=first):
                    for owner in (first, first + 1):
                        wait_block(1, jnp.where(in_left, owner, visits - 1 - owner))

        for j, block in enumerate(blocks_of(pair)):
            three = jnp.concatenate([window[block + k] for k in range(3)], 1)
            three = pltpu.roll(three, 2 * LANES + SHIFT, 1)[:, :PAIR]
            high, low = split(three)
            which = jnp.where(block == 0, 1, jnp.where(block == blocks - 1, 2, 0))
            field = (
                dot(high, col_ops[which, 0])
                + dot(low, col_ops[which, 0])
                + dot(high, col_ops[which, 1])
            )
            out = slice(j * LANES, (j + 1) * LANES)
            for f in range(2 * N_COL):
                for part in range(2):
                    first = part * lower_start(rows)
                    h, l = split(field[first : first + reach, f * LANES : (f + 1) * LANES])
                    stage[f, part, 0:reach, out] = h
                    stage[f, part, reach : 2 * reach, out] = l
                    stage[f, part, 2 * reach : 3 * reach, out] = h
        for part in range(2):
            into = slice(part * (rows // 2), (part + 1) * (rows // 2))
            for f in range(2 * N_COL):
                made = [b + BASIS * (f // N_COL) for b in range(BASIS) if COL_OF[b] == f % N_COL]
                ops = [row_ops[part, at] for at in made]
                ops = ops[0] if len(ops) == 1 else jnp.concatenate(ops, 0)
                image = dot(ops, stage[f, part])
                for k, at in enumerate(made):
                    fields[pair, at, into, :] = image[k * (rows // 2) : (k + 1) * (rows // 2)]

        def gather(slab, acc):
            at = pl.ds(pl.multiple_of(slab * 8, 8), 8)
            acc = list(acc)
            for j, block in enumerate(blocks_of(pair)):
                cut_at = slice(j * LANES, (j + 1) * LANES)
                m = [fields[pair, b, at, cut_at] for b in range(BASIS)]
                s = science[at, lane(block + 1)]
                terms = [m[b] * m[c] for b in range(BASIS) for c in range(b, BASIS)]
                terms += m + [m[b] * s for b in range(BASIS)] + [s]
                acc = [a + t for a, t in zip(acc, terms)]
            return tuple(acc)

        acc = tuple(sums[k] for k in range(N_SUMS))
        acc = lax.fori_loop(0, rows // 8, gather, acc, unroll=4)
        for k in range(N_SUMS):
            sums[k] = acc[k]
        return carry

    lax.fori_loop(0, pairs, exposure_pair, 0)

    totals[group] = jnp.sum(sums[...], axis=1)

    def total_copy(step, source=None):
        source = group if source is None else source
        return pltpu.make_async_remote_copy(
            src_ref=totals.at[source],
            dst_ref=totals.at[source],
            send_sem=total_send.at[step],
            recv_sem=total_recv.at[source],
            device_id=(me, lax.rem(group + step, groups)),
            device_id_type=MESH,
        )

    for step in range(1, groups):
        total_copy(step).start()
    for step in range(1, groups):
        total_copy(step, lax.rem(group + step, groups)).wait_recv()
    total = totals[0]
    for g in range(1, groups):
        total = total + totals[g]
    counted = float(rows * cols * groups)
    total = jnp.sum(total, axis=1, keepdims=True) / counted
    entry = [jnp.broadcast_to(total[k : k + 1, :], (8, LANES)) for k in range(N_SUMS)]

    size = BASIS + 1
    normal = {}
    at = 0
    for b in range(BASIS):
        for c in range(b, BASIS):
            normal[b, c] = entry[at] + RIDGE if b == c else entry[at]
            at += 1
    for b in range(BASIS):
        normal[b, BASIS] = entry[at + b]
    normal[BASIS, BASIS] = jnp.full((8, LANES), 1.0 + RIDGE, jnp.float32)
    rhs = [entry[at + BASIS + b] for b in range(size)]
    inverse = []
    for k in range(size):
        inverse.append(1.0 / normal[k, k])
        for i in range(k + 1, size):
            factor = normal[k, i] * inverse[k]
            for j in range(i, size):
                normal[i, j] = normal[i, j] - factor * normal[k, j]
            rhs[i] = rhs[i] - factor * rhs[k]
    coef = [None] * size
    for k in reversed(range(size)):
        value = rhs[k]
        for j in range(k + 1, size):
            value = value - normal[k, j] * coef[j]
        coef[k] = value * inverse[k]

    def combine(slab, power):
        at = pl.ds(pl.multiple_of(slab * 8, 8), 8)
        edge = coef[BASIS] * ones_rows[at, :]
        for block in range(blocks):
            pair, j = pair_of(block)
            cut_at = slice(j * LANES, (j + 1) * LANES)
            even_at = slice(block % 2 * LANES, (block % 2 + 1) * LANES)
            first = block * LANES
            s = science[at, first + LANES : first + 2 * LANES]
            f = smoothed[block // 2, at, even_at] - edge * ones_cols[:, first : first + LANES]
            m = coef[0] * fields[pair, 0, at, cut_at]
            g = coef[0] * fields[pair, BASIS, at, cut_at]
            for b in range(1, BASIS):
                m = m + coef[b] * fields[pair, b, at, cut_at]
                g = g + coef[b] * fields[pair, BASIS + b, at, cut_at]
            partial = s - m
            whole = partial - coef[BASIS]
            difference_ref[at, first : first + LANES] = whole
            filtered_ref[at, first : first + LANES] = f - g
            power = power + whole * whole
        return power

    power = lax.fori_loop(0, rows // 8, combine, jnp.zeros((8, LANES), jnp.float32))
    power = jnp.sum(jnp.sum(power, axis=1, keepdims=True), axis=0, keepdims=True)
    scale = 1.0 / jnp.sqrt(power / float(rows * cols) + EPSILON)
    column = lax.broadcasted_iota(jnp.int32, (8, LANES), 1)
    row = lax.broadcasted_iota(jnp.int32, (8, LANES), 0)
    small = jnp.broadcast_to(scale, (8, LANES))
    for k in range(size):
        small = jnp.where((row == 0) & (column == k), coef[k], small)
    small_ref[...] = small

    for step in range(1, visits):
        place_copy(step).wait_send()
        for chunk in range(chunks):
            first_copy(chunk, step).wait_send()
            second_copy(chunk, step).wait_send()
    for step in range(1, groups):
        total_copy(step).wait_send()

    @pl.when(has_right)
    def _():
        science_right.wait_send()
        window_right.wait_send()

    @pl.when(has_left)
    def _():
        science_left.wait_send()
        window_left.wait_send()


def finish(difference, filtered, small, difference_ref, significance_ref, coef_ref, scaled, sems, sem):
    out = pltpu.make_async_copy(difference, difference_ref, sem)
    out.start()
    scale = small[1:2, 0:1]
    size = difference.shape[0] // PARTS
    copies = []
    for part in range(PARTS):
        at = pl.ds(part * size, size)
        scaled[part] = filtered[at, :] * scale
        copies.append(
            pltpu.make_async_copy(scaled.at[part], significance_ref.at[at, :], sems.at[part])
        )
        copies[-1].start()
    coef_ref[...] = small[0:1, 0 : BASIS + 1]
    out.wait()
    for copy in copies:
        copy.wait()


def shards(coadd_tiles, science, correlation, offset):
    visits = lax.axis_size("visit")
    groups = lax.axis_size("grp")
    rows, cols = coadd_tiles.shape
    blocks = cols // LANES
    pairs = blocks // 2
    chunks = blocks // visits
    span = rows + 2 * KER_HALF
    sent = span
    depth = -(-span // 16) * 16
    reach = -(-sent // 8) * 8 - lower_start(rows)
    consts = constants(rows, cols, groups, reach)
    row_ops, smooth_op, col_ops, smooth_cols, ones_rows, ones_cols = consts
    f32, bf16 = jnp.float32, jnp.bfloat16
    anywhere = pl.BlockSpec(memory_space=pl.ANY)
    scalar = pl.BlockSpec(memory_space=pltpu.SMEM)
    vmem = pl.BlockSpec(memory_space=pltpu.VMEM)
    dma = pltpu.SemaphoreType.DMA
    difference, filtered, small = pl.pallas_call(
        functools.partial(kernel, visits, groups),
        out_shape=(
            pltpu.VMEM((rows, cols), f32),
            pltpu.VMEM((rows, cols), f32),
            pltpu.VMEM((8, LANES), f32),
        ),
        in_specs=[anywhere, anywhere, scalar, scalar] + [anywhere] * 6,
        out_specs=(vmem, vmem, vmem),
        scratch_shapes=[
            (pltpu.VMEM((visits * rows + sent, LANES), f32),) * chunks,
            pltpu.VMEM((chunks, visits, sent, LANES), f32),
            pltpu.VMEM((blocks + 2, depth, LANES), f32),
            pltpu.VMEM((rows, cols + 2 * LANES), f32),
            pltpu.VMEM((pairs, 2 * BASIS, rows, PAIR), f32),
            pltpu.VMEM((2 * N_COL, 2, 3 * reach, PAIR), bf16),
            pltpu.VMEM((3 * rows, PAIR), bf16),
            pltpu.VMEM((pairs, rows, PAIR), f32),
            pltpu.VMEM((32, 8, LANES), f32),
            pltpu.VMEM((groups, 32, LANES), f32),
            pltpu.VMEM((8, LANES), jnp.int32),
            pltpu.VMEM((visits, 8, LANES), jnp.int32),
            pltpu.VMEM(row_ops.shape, bf16),
            pltpu.VMEM(smooth_op.shape, bf16),
            pltpu.VMEM(col_ops.shape, bf16),
            pltpu.VMEM(smooth_cols.shape, bf16),
            pltpu.VMEM(ones_rows.shape, f32),
            pltpu.VMEM(ones_cols.shape[1:], f32),
            dma((9 + chunks,)),
            dma((visits,)),
            dma((visits,)),
            dma((chunks, visits)),
            dma((chunks, visits)),
            dma((chunks, visits)),
            dma((chunks, visits)),
            dma((4,)),
            dma((4,)),
            dma((groups,)),
            dma((groups,)),
        ],
        compiler_params=pltpu.CompilerParams(
            collective_id=0, has_side_effects=True, vmem_limit_bytes=54 * 1024 * 1024
        ),
        name="difference_imaging",
    )(coadd_tiles, science, correlation, offset, *[jnp.asarray(c) for c in consts])
    return pl.pallas_call(
        finish,
        out_shape=(
            jax.ShapeDtypeStruct((rows, cols), f32),
            jax.ShapeDtypeStruct((rows, cols), f32),
            jax.ShapeDtypeStruct((1, BASIS + 1), f32),
        ),
        in_specs=[vmem] * 3,
        out_specs=(anywhere, anywhere, vmem),
        scratch_shapes=[
            pltpu.VMEM((PARTS, rows // PARTS, cols), f32),
            dma((PARTS,)),
            dma,
        ],
        compiler_params=pltpu.CompilerParams(vmem_limit_bytes=8 * 1024 * 1024),
        name="finish",
    )(*[pltpu.with_memory_space_constraint(x, pltpu.VMEM) for x in (difference, filtered, small)])


def solution(mesh):
    in_specs = (P("visit", "grp"), P("visit", "grp"), P("visit"), P("visit"))
    out_specs = (P("visit", "grp"), P("visit", "grp"), P("visit", None))
    return jax.shard_map(shards, mesh=mesh, in_specs=in_specs, out_specs=out_specs, check_vma=False)
```
